256 devices in a mesh: rows: 32 (over z, y_lo, core), chan: 8 (over x, y_hi).
Axes of the slice: x: 4, y: 4 (y_hi: 2, y_lo: 2; y = y_hi * 2 + y_lo), z: 8, core: 2. Of those that a mesh axis runs over, the one named last changes fastest.
Arguments:
- frame_one: bfloat16 [8192, 256], P('rows', 'chan'), may hold values from -6 to 6
- frame_two: bfloat16 [256, 480, 256], P('rows', None, 'chan'), may hold values from -6 to 6
Outputs:
- pyramid: bfloat16 [32, 5040, 8192], P(None, 'chan', 'rows')
The draws below stay inside these ranges and needn't reach their ends.
All inputs are finite; a program needn't handle non-finite values.
Results may differ from the reference program's by a relative error of at most 0.0016.
Values may be sent and summed in bfloat16 or wider, within the bound.
A program may use at most 128 MiB of HBM per device.

```python
import jax
import jax.numpy as jnp
from jax import lax

C = 256
W = 480
SR = 8
Q = 8192
NS = 32
H2 = 256


def block_levels(stream_key, shape, split, least, top_value):
    level, own = 1.0, jax.random.fold_in(stream_key, 6)
    for axis_at, blocks in split:
        steps = jnp.exp(jax.random.uniform(jax.random.fold_in(own, axis_at), (blocks,), jnp.float32, least / len(split), top_value / len(split)))
        level = level * jnp.repeat(steps, shape[axis_at] // blocks).reshape([-1 if axis == axis_at else 1 for axis in range(len(shape))])
    return level


def noise(rng, dims, deviation, limit, shards=(), dtype=jnp.bfloat16):
    entries = jax.random.normal(rng, dims, jnp.float32) * deviation
    if len(shards) > 0:
        entries = block_levels(rng, dims, shards, -0.22, 0.18) * entries
    return jnp.clip(entries, min=-limit, max=limit).astype(dtype)


def setup_inputs(seed: int = 0) -> dict:
    key_of = jax.random.split(jax.random.key(seed), 3)
    frame_one = noise(key_of[0], (Q, C), 1.0, 6.0, ((0, 32), (1, 8)))
    frame_two = noise(key_of[1], (H2, W, C), 1.0, 6.0, ((0, 32), (2, 8)))
    return dict(frame_one=frame_one, frame_two=frame_two)


def pool_strip(strip):
    full = strip.astype(jnp.float32)
    rows_n, cols_n, chans = full.shape
    level_one = full.reshape(rows_n // 2, 2, cols_n // 2, 2, chans).mean(axis=(1, 3))
    level_two = level_one.reshape(rows_n // 4, 2, cols_n // 4, 2, chans).mean(axis=(1, 3))
    joined = jnp.concatenate([full.reshape(-1, chans), level_one.reshape(-1, chans), level_two.reshape(-1, chans)], axis=0)
    return joined.astype(jnp.bfloat16)

def reference(frame_one, frame_two):
    strips = frame_two.reshape(NS, SR, W, C)
    factor = 1.0 / jnp.sqrt(jnp.float32(C))

    def one_strip(strip):
        pooled = pool_strip(strip)
        values = lax.dot_general(pooled, frame_one, (((1,), (1,)), ((), ())), preferred_element_type=jnp.float32)
        return (values * factor).astype(jnp.bfloat16)
    return lax.map(one_strip, strips)
```

```python
import jax
import jax.numpy as jnp
from jax import lax
from jax.sharding import PartitionSpec as P


def pool_strip(strip):
    full = strip.astype(jnp.float32)
    rows_n, cols_n, chans = full.shape
    level_one = full.reshape(rows_n // 2, 2, cols_n // 2, 2, chans).mean(axis=(1, 3))
    level_two = level_one.reshape(rows_n // 4, 2, cols_n // 4, 2, chans).mean(axis=(1, 3))
    joined = jnp.concatenate(
        [full.reshape(-1, chans), level_one.reshape(-1, chans), level_two.reshape(-1, chans)],
        axis=0,
    )
    return joined.astype(jnp.bfloat16)


def local(frame_one, frame_two):
    queries = lax.all_gather(frame_one, "chan", axis=1, tiled=True)
    channels = queries.shape[1]
    factor = 1.0 / jnp.sqrt(jnp.float32(channels))
    pooled = pool_strip(frame_two)
    groups = lax.axis_size("chan")
    share = pooled.shape[0] // groups
    slices = pooled.shape[1]
    blocks = pooled.reshape(groups, share, slices)
    traded = lax.all_to_all(blocks, "chan", split_axis=0, concat_axis=0, tiled=True)
    gathered = lax.all_gather(traded, "rows", axis=0, tiled=False)
    split_queries = queries.reshape(queries.shape[0], groups, slices)
    values = jnp.einsum("skpc,qkc->psq", gathered, split_queries, preferred_element_type=jnp.float32)
    values = (values * factor).astype(jnp.bfloat16)
    return jnp.transpose(values, (1, 0, 2))


def solution(mesh):
    in_specs = (P("rows", "chan"), P("rows", None, "chan"))
    out_specs = P(None, "chan", "rows")
    return jax.shard_map(local, mesh=mesh, in_specs=in_specs, out_specs=out_specs, check_vma=False)
```

```python
import jax
import jax.numpy as jnp
from jax import lax
from jax.sharding import Mesh, PartitionSpec as P


def pool_strip(strip):
    full = strip.astype(jnp.float32)
    rows_n, cols_n, chans = full.shape
    level_one = full.reshape(rows_n // 2, 2, cols_n // 2, 2, chans).mean(axis=(1, 3))
    level_two = level_one.reshape(rows_n // 4, 2, cols_n // 4, 2, chans).mean(axis=(1, 3))
    joined = jnp.concatenate(
        [full.reshape(-1, chans), level_one.reshape(-1, chans), level_two.reshape(-1, chans)],
        axis=0,
    )
    return joined.astype(jnp.bfloat16)


def local(frame_one, frame_two):
    queries = lax.all_gather(frame_one, "chan", axis=1, tiled=True)
    channels = queries.shape[1]
    factor = 1.0 / jnp.sqrt(jnp.float32(channels))
    pooled = pool_strip(frame_two)
    groups = lax.axis_size("chan")
    cores = lax.axis_size("core")
    share = pooled.shape[0] // groups
    slices = pooled.shape[1]
    blocks = pooled.reshape(groups, share, slices)
    traded = lax.all_to_all(blocks, "chan", split_axis=0, concat_axis=0, tiled=True)
    halves = traded.reshape(cores, groups // cores, share, slices)
    mine = lax.all_to_all(halves, "core", split_axis=0, concat_axis=0, tiled=True)
    gathered = lax.all_gather(mine, "grp", axis=0, tiled=False)
    both = lax.all_gather(gathered, "core", axis=0, tiled=False)
    split_queries = queries.reshape(queries.shape[0], cores, groups // cores, slices)
    values = jnp.einsum("hgrkpc,qhkc->pgrq", both, split_queries, preferred_element_type=jnp.float32)
    values = (values * factor).astype(jnp.bfloat16)
    values = values.reshape(share, -1, values.shape[-1])
    return jnp.transpose(values, (1, 0, 2))


def solution(mesh):
    rows = mesh.shape["rows"]
    devices = mesh.devices.reshape(rows // 2, 2, mesh.shape["chan"])
    fine = Mesh(devices, ("grp", "core", "chan"))
    strips = ("grp", "core")
    in_specs = (P(strips, "chan"), P(strips, None, "chan"))
    out_specs = P(None, "chan", strips)
    return jax.shard_map(local, mesh=fine, in_specs=in_specs, out_specs=out_specs, check_vma=False)
```

```python
import functools

import jax
import jax.numpy as jnp
from jax import lax
from jax.experimental import pallas as pl
from jax.experimental.pallas import tpu as pltpu
from jax.sharding import PartitionSpec as P


def pool_strip(strip):
    full = strip.astype(jnp.float32)
    rows_n, cols_n, chans = full.shape
    level_one = full.reshape(rows_n // 2, 2, cols_n // 2, 2, chans).mean(axis=(1, 3))
    level_two = level_one.reshape(rows_n // 4, 2, cols_n // 4, 2, chans).mean(axis=(1, 3))
    joined = jnp.concatenate(
        [full.reshape(-1, chans), level_one.reshape(-1, chans), level_two.reshape(-1, chans)],
        axis=0,
    )
    return joined.astype(jnp.bfloat16)


def correlate_kernel(factor, x_ref, f_ref, o_ref):
    for s in range(x_ref.shape[0]):
        acc = lax.dot_general(
            x_ref[s], f_ref[...], (((1,), (1,)), ((), ())), preferred_element_type=jnp.float32
        )
        o_ref[:, s, :] = (acc * factor).astype(o_ref.dtype)


def correlate(gathered, queries, factor, strips_per_step=16, rows_per_step=128):
    strips, share, chans = gathered.shape
    width = queries.shape[0]
    grid = (pl.cdiv(share, rows_per_step), strips // strips_per_step)
    return pl.pallas_call(
        functools.partial(correlate_kernel, factor),
        out_shape=jax.ShapeDtypeStruct((share, strips, width), jnp.bfloat16),
        grid=grid,
        in_specs=[
            pl.BlockSpec((strips_per_step, rows_per_step, chans), lambda i, j: (j, i, 0)),
            pl.BlockSpec((width, chans), lambda i, j: (0, 0)),
        ],
        out_specs=pl.BlockSpec((rows_per_step, strips_per_step, width), lambda i, j: (i, j, 0)),
        cost_estimate=pl.CostEstimate(
            flops=2 * strips * share * chans * width,
            bytes_accessed=2 * (strips * share * chans + width * chans + strips * share * width),
            transcendentals=0,
        ),
    )(gathered, queries)


def local(frame_one, frame_two):
    queries = lax.all_gather(frame_one, "chan", axis=1, tiled=True)
    channels = queries.shape[1]
    factor = 1.0 / float(channels) ** 0.5
    pooled = pool_strip(frame_two)
    groups = lax.axis_size("chan")
    share = pooled.shape[0] // groups
    slices = pooled.shape[1]
    blocks = pooled.reshape(groups, share, slices)
    traded = lax.all_to_all(blocks, "chan", split_axis=0, concat_axis=0, tiled=True)
    traded = jnp.transpose(traded, (1, 0, 2)).reshape(share, groups * slices)
    gathered = lax.all_gather(traded, "rows", axis=0, tiled=False)
    strips = gathered.shape[0]
    values = correlate(gathered, queries, factor)
    return jnp.transpose(values, (1, 0, 2))


def solution(mesh):
    in_specs = (P("rows", "chan"), P("rows", None, "chan"))
    out_specs = P(None, "chan", "rows")
    return jax.shard_map(local, mesh=mesh, in_specs=in_specs, out_specs=out_specs, check_vma=False)
```

```python
import functools

import jax
import jax.numpy as jnp
from jax import lax
from jax.experimental import pallas as pl
from jax.experimental.pallas import tpu as pltpu
from jax.sharding import Mesh, PartitionSpec as P


def pool_strip(strip):
    full = strip.astype(jnp.float32)
    rows_n, cols_n, chans = full.shape
    level_one = full.reshape(rows_n // 2, 2, cols_n // 2, 2, chans).mean(axis=(1, 3))
    level_two = level_one.reshape(rows_n // 4, 2, cols_n // 4, 2, chans).mean(axis=(1, 3))
    joined = jnp.concatenate(
        [full.reshape(-1, chans), level_one.reshape(-1, chans), level_two.reshape(-1, chans)],
        axis=0,
    )
    return joined.astype(jnp.bfloat16)


def correlate_kernel(factor, x_ref, f_ref, o_ref):
    for s in range(x_ref.shape[0]):
        acc = lax.dot_general(
            x_ref[s], f_ref[...], (((1,), (1,)), ((), ())), preferred_element_type=jnp.float32
        )
        o_ref[:, s, :] = (acc * factor).astype(o_ref.dtype)


def correlate(gathered, queries, factor, share, rows_per_step=160):
    halves, strips, half_rows, chans = gathered.shape
    width = queries.shape[0]
    per_half = half_rows // rows_per_step
    grid = (pl.cdiv(share, rows_per_step),)
    return pl.pallas_call(
        functools.partial(correlate_kernel, factor),
        out_shape=jax.ShapeDtypeStruct((share, strips, width), jnp.bfloat16),
        grid=grid,
        in_specs=[
            pl.BlockSpec((None, strips, rows_per_step, chans), lambda i: (i // per_half, 0, i % per_half, 0)),
            pl.BlockSpec((width, chans), lambda i: (0, 0)),
        ],
        out_specs=pl.BlockSpec((rows_per_step, strips, width), lambda i: (i, 0, 0)),
        cost_estimate=pl.CostEstimate(
            flops=2 * strips * share * chans * width,
            bytes_accessed=2 * (strips * share * chans + width * chans + strips * share * width),
            transcendentals=0,
        ),
    )(gathered, queries)


def local(frame_one, frame_two):
    groups = lax.axis_size("chan")
    cores = lax.axis_size("core")
    pieces = lax.all_gather(frame_one, "chan", axis=0, tiled=False)
    queries = jnp.transpose(pieces, (1, 0, 2)).reshape(frame_one.shape[0], -1)
    channels = queries.shape[1]
    factor = 1.0 / float(channels) ** 0.5
    pooled = pool_strip(frame_two)
    share = pooled.shape[0] // groups
    slices = pooled.shape[1]
    blocks = pooled.reshape(groups, share, slices)
    traded = lax.all_to_all(blocks, "chan", split_axis=0, concat_axis=0, tiled=True)
    traded = jnp.transpose(traded, (1, 0, 2)).reshape(share, channels)
    padded_rows = -(-share // (16 * cores)) * 16 * cores
    traded = jnp.pad(traded, ((0, padded_rows - share), (0, 0)))
    halves = traded.reshape(cores, padded_rows // cores, channels)
    mine = lax.all_to_all(halves, "core", split_axis=0, concat_axis=0, tiled=False)
    pair = lax.all_gather(mine, "ylo", axis=0, tiled=False)
    ring = lax.all_gather(pair, "z", axis=0, tiled=False)
    ring = ring.reshape(-1, padded_rows // cores, channels)
    both = lax.all_gather(ring, "core", axis=0, tiled=False)
    values = correlate(both, queries, factor, share)
    return jnp.transpose(values, (1, 0, 2))


def solution(mesh):
    z = 8
    rows = mesh.shape["rows"]
    devices = mesh.devices.reshape(z, rows // (2 * z), 2, mesh.shape["chan"])
    fine = Mesh(devices, ("z", "ylo", "core", "chan"))
    strips = ("z", "ylo", "core")
    in_specs = (P(strips, "chan"), P(strips, None, "chan"))
    out_specs = P(None, "chan", strips)
    return jax.shard_map(local, mesh=fine, in_specs=in_specs, out_specs=out_specs, check_vma=False)
```

```python
import functools

import jax
import jax.numpy as jnp
from jax import lax
from jax.experimental import pallas as pl
from jax.experimental.pallas import tpu as pltpu
from jax.sharding import PartitionSpec as P

MESH_ID = pl.DeviceIdType.MESH


def pool_strip(strip):
    full = strip.astype(jnp.float32)
    rows_n, cols_n, chans = full.shape
    level_one = full.reshape(rows_n // 2, 2, cols_n // 2, 2, chans).mean(axis=(1, 3))
    level_two = level_one.reshape(rows_n // 4, 2, cols_n // 4, 2, chans).mean(axis=(1, 3))
    joined = jnp.concatenate(
        [full.reshape(-1, chans), level_one.reshape(-1, chans), level_two.reshape(-1, chans)],
        axis=0,
    )
    return joined.astype(jnp.bfloat16)


def trade_kernel(n, x_ref, o_ref, buf, send_sem, recv_sem):
    me = lax.axis_index("chan")
    row = lax.axis_index("rows")
    barrier = pltpu.get_barrier_semaphore()
    for k in range(1, n):
        peer = lax.rem(me + k, n)
        pl.semaphore_signal(barrier, inc=1, device_id=(row, peer), device_id_type=MESH_ID)
    pl.semaphore_wait(barrier, n - 1)
    sends = []
    for k in range(1, n):
        peer = lax.rem(me + k, n)
        copy = pltpu.make_async_remote_copy(
            src_ref=x_ref.at[peer],
            dst_ref=buf.at[me],
            send_sem=send_sem.at[k],
            recv_sem=recv_sem.at[k],
            device_id=(row, peer),
            device_id_type=MESH_ID,
        )
        copy.start()
        sends.append(copy)
    o_ref[me] = x_ref[me]
    for k in range(1, n):
        source = lax.rem(me + n - k, n)
        arrival = pltpu.make_async_remote_copy(
            src_ref=x_ref.at[me],
            dst_ref=buf.at[source],
            send_sem=send_sem.at[k],
            recv_sem=recv_sem.at[k],
            device_id=(row, source),
            device_id_type=MESH_ID,
        )
        arrival.wait_recv()
        o_ref[source] = buf[source]
    for copy in sends:
        copy.wait_send()


def trade(blocks):
    n = blocks.shape[0]
    return pl.pallas_call(
        functools.partial(trade_kernel, n),
        out_shape=jax.ShapeDtypeStruct(blocks.shape, blocks.dtype),
        in_specs=[pl.BlockSpec(memory_space=pltpu.VMEM)],
        out_specs=pl.BlockSpec(memory_space=pltpu.VMEM),
        scratch_shapes=[
            pltpu.VMEM(blocks.shape, blocks.dtype),
            pltpu.SemaphoreType.DMA((n,)),
            pltpu.SemaphoreType.DMA((n,)),
        ],
        compiler_params=pltpu.CompilerParams(collective_id=0, has_side_effects=True),
    )(blocks)


def correlate_kernel(factor, x_ref, f_ref, o_ref):
    for s in range(x_ref.shape[0]):
        acc = lax.dot_general(
            x_ref[s], f_ref[...], (((1,), (1,)), ((), ())), preferred_element_type=jnp.float32
        )
        o_ref[:, s, :] = (acc * factor).astype(o_ref.dtype)


def correlate(gathered, queries, factor, strips_per_step=16, rows_per_step=128):
    strips, share, chans = gathered.shape
    width = queries.shape[0]
    grid = (pl.cdiv(share, rows_per_step), strips // strips_per_step)
    return pl.pallas_call(
        functools.partial(correlate_kernel, factor),
        out_shape=jax.ShapeDtypeStruct((share, strips, width), jnp.bfloat16),
        grid=grid,
        in_specs=[
            pl.BlockSpec((strips_per_step, rows_per_step, chans), lambda i, j: (j, i, 0)),
            pl.BlockSpec((width, chans), lambda i, j: (0, 0)),
        ],
        out_specs=pl.BlockSpec((rows_per_step, strips_per_step, width), lambda i, j: (i, j, 0)),
        cost_estimate=pl.CostEstimate(
            flops=2 * strips * share * chans * width,
            bytes_accessed=2 * (strips * share * chans + width * chans + strips * share * width),
            transcendentals=0,
        ),
    )(gathered, queries)


def local(frame_one, frame_two):
    queries = lax.all_gather(frame_one, "chan", axis=1, tiled=True)
    channels = queries.shape[1]
    factor = 1.0 / float(channels) ** 0.5
    pooled = pool_strip(frame_two)
    groups = lax.axis_size("chan")
    share = pooled.shape[0] // groups
    slices = pooled.shape[1]
    blocks = jnp.transpose(pooled.reshape(groups, share, slices), (0, 2, 1))
    traded = trade(blocks)
    traded = jnp.transpose(traded, (2, 0, 1)).reshape(share, channels)
    gathered = lax.all_gather(traded, "rows", axis=0, tiled=False)
    values = correlate(gathered, queries, factor)
    return jnp.transpose(values, (1, 0, 2))


def solution(mesh):
    in_specs = (P("rows", "chan"), P("rows", None, "chan"))
    out_specs = P(None, "chan", "rows")
    return jax.shard_map(local, mesh=mesh, in_specs=in_specs, out_specs=out_specs, check_vma=False)
```

```python
import functools

import jax
import jax.numpy as jnp
from jax import lax
from jax.experimental import pallas as pl
from jax.experimental.pallas import tpu as pltpu
from jax.sharding import PartitionSpec as P

MESH_ID = pl.DeviceIdType.MESH


def pool_strip(strip):
    full = strip.astype(jnp.float32)
    rows_n, cols_n, chans = full.shape
    level_one = full.reshape(rows_n // 2, 2, cols_n // 2, 2, chans).mean(axis=(1, 3))
    level_two = level_one.reshape(rows_n // 4, 2, cols_n // 4, 2, chans).mean(axis=(1, 3))
    joined = jnp.concatenate(
        [full.reshape(-1, chans), level_one.reshape(-1, chans), level_two.reshape(-1, chans)],
        axis=0,
    )
    return joined.astype(jnp.bfloat16)


def trade_kernel(n, x_ref, o_ref, buf, send_sem, recv_sem):
    me = lax.axis_index("chan")
    row = lax.axis_index("rows")
    barrier = pltpu.get_barrier_semaphore()
    for k in range(1, n):
        peer = lax.rem(me + k, n)
        pl.semaphore_signal(barrier, inc=1, device_id=(row, peer), device_id_type=MESH_ID)
    pl.semaphore_wait(barrier, n - 1)
    sends = []
    for k in range(1, n):
        peer = lax.rem(me + k, n)
        copy = pltpu.make_async_remote_copy(
            src_ref=x_ref.at[peer],
            dst_ref=buf.at[me],
            send_sem=send_sem.at[k],
            recv_sem=recv_sem.at[k],
            device_id=(row, peer),
            device_id_type=MESH_ID,
        )
        copy.start()
        sends.append(copy)
    o_ref[me] = x_ref[me]
    for k in range(1, n):
        source = lax.rem(me + n - k, n)
        arrival = pltpu.make_async_remote_copy(
            src_ref=x_ref.at[me],
            dst_ref=buf.at[source],
            send_sem=send_sem.at[k],
            recv_sem=recv_sem.at[k],
            device_id=(row, source),
            device_id_type=MESH_ID,
        )
        arrival.wait_recv()
        o_ref[source] = buf[source]
    for copy in sends:
        copy.wait_send()


def trade(blocks):
    n = blocks.shape[0]
    return pl.pallas_call(
        functools.partial(trade_kernel, n),
        out_shape=jax.ShapeDtypeStruct(blocks.shape, blocks.dtype),
        in_specs=[pl.BlockSpec(memory_space=pltpu.VMEM)],
        out_specs=pl.BlockSpec(memory_space=pltpu.VMEM),
        scratch_shapes=[
            pltpu.VMEM(blocks.shape, blocks.dtype),
            pltpu.SemaphoreType.DMA((n,)),
            pltpu.SemaphoreType.DMA((n,)),
        ],
        compiler_params=pltpu.CompilerParams(collective_id=0, has_side_effects=True),
    )(blocks)


def correlate_kernel(factor, x_ref, f_ref, o_ref):
    for s in range(x_ref.shape[0]):
        acc = jnp.dot(x_ref[s], f_ref[...], preferred_element_type=jnp.float32)
        o_ref[:, s, :] = (acc * factor).astype(o_ref.dtype)


def correlate(gathered, queries, factor, strips_per_step=32, rows_per_step=128):
    strips, share, chans = gathered.shape
    width = queries.shape[1]
    grid = (pl.cdiv(share, rows_per_step), strips // strips_per_step)
    return pl.pallas_call(
        functools.partial(correlate_kernel, factor),
        out_shape=jax.ShapeDtypeStruct((share, strips, width), jnp.bfloat16),
        grid=grid,
        in_specs=[
            pl.BlockSpec((strips_per_step, rows_per_step, chans), lambda i, j: (j, i, 0)),
            pl.BlockSpec((chans, width), lambda i, j: (0, 0)),
        ],
        out_specs=pl.BlockSpec((rows_per_step, strips_per_step, width), lambda i, j: (i, j, 0)),
        cost_estimate=pl.CostEstimate(
            flops=2 * strips * share * chans * width,
            bytes_accessed=2 * (strips * share * chans + width * chans + strips * share * width),
            transcendentals=0,
        ),
    )(gathered, queries)


def local(frame_one, frame_two):
    queries = lax.all_gather(frame_one, "chan", axis=1, tiled=True)
    channels = queries.shape[1]
    factor = 1.0 / float(channels) ** 0.5
    pooled = pool_strip(frame_two)
    groups = lax.axis_size("chan")
    share = pooled.shape[0] // groups
    slices = pooled.shape[1]
    blocks = jnp.transpose(pooled.reshape(groups, share, slices), (0, 2, 1))
    traded = trade(blocks)
    traded = jnp.transpose(traded, (2, 0, 1)).reshape(share, channels)
    gathered = lax.all_gather(traded, "rows", axis=0, tiled=False)
    values = correlate(gathered, queries.T, factor)
    return jnp.transpose(values, (1, 0, 2))


def solution(mesh):
    in_specs = (P("rows", "chan"), P("rows", None, "chan"))
    out_specs = P(None, "chan", "rows")
    return jax.shard_map(local, mesh=mesh, in_specs=in_specs, out_specs=out_specs, check_vma=False)
```

```python
import functools

import jax
import jax.numpy as jnp
from jax import lax
from jax.experimental import pallas as pl
from jax.experimental.pallas import tpu as pltpu
from jax.sharding import PartitionSpec as P

MESH_ID = pl.DeviceIdType.MESH


def pool_strip(strip):
    full = strip.astype(jnp.float32)
    rows_n, cols_n, chans = full.shape
    level_one = full.reshape(rows_n // 2, 2, cols_n // 2, 2, chans).mean(axis=(1, 3))
    level_two = level_one.reshape(rows_n // 4, 2, cols_n // 4, 2, chans).mean(axis=(1, 3))
    joined = jnp.concatenate(
        [full.reshape(-1, chans), level_one.reshape(-1, chans), level_two.reshape(-1, chans)],
        axis=0,
    )
    return joined.astype(jnp.bfloat16)


def trade_kernel(n, x_ref, o_ref, buf, send_sem, recv_sem):
    me = lax.axis_index("chan")
    row = lax.axis_index("rows")
    barrier = pltpu.get_barrier_semaphore()
    for k in range(1, n):
        peer = lax.rem(me + k, n)
        pl.semaphore_signal(barrier, inc=1, device_id=(row, peer), device_id_type=MESH_ID)
    pl.semaphore_wait(barrier, n - 1)
    sends = []
    for k in range(1, n):
        peer = lax.rem(me + k, n)
        copy = pltpu.make_async_remote_copy(
            src_ref=x_ref.at[peer],
            dst_ref=buf.at[me],
            send_sem=send_sem.at[k],
            recv_sem=recv_sem.at[k],
            device_id=(row, peer),
            device_id_type=MESH_ID,
        )
        copy.start()
        sends.append(copy)
    o_ref[me] = x_ref[me]
    for k in range(1, n):
        source = lax.rem(me + n - k, n)
        arrival = pltpu.make_async_remote_copy(
            src_ref=x_ref.at[me],
            dst_ref=buf.at[source],
            send_sem=send_sem.at[k],
            recv_sem=recv_sem.at[k],
            device_id=(row, source),
            device_id_type=MESH_ID,
        )
        arrival.wait_recv()
        o_ref[source] = buf[source]
    for copy in sends:
        copy.wait_send()


def trade(blocks):
    n = blocks.shape[0]
    return pl.pallas_call(
        functools.partial(trade_kernel, n),
        out_shape=jax.ShapeDtypeStruct(blocks.shape, blocks.dtype),
        in_specs=[pl.BlockSpec(memory_space=pltpu.VMEM)],
        out_specs=pl.BlockSpec(memory_space=pltpu.VMEM),
        scratch_shapes=[
            pltpu.VMEM(blocks.shape, blocks.dtype),
            pltpu.SemaphoreType.DMA((n,)),
            pltpu.SemaphoreType.DMA((n,)),
        ],
        compiler_params=pltpu.CompilerParams(collective_id=0, has_side_effects=True),
    )(blocks)


def correlate_kernel(factor, x_ref, f_ref, *refs):
    o_ref = refs[-1]
    for s in range(x_ref.shape[0]):
        acc = jnp.dot(x_ref[s], f_ref[...], preferred_element_type=jnp.float32)
        o_ref[:, s, :] = (acc * factor).astype(o_ref.dtype)


def correlate(gathered, queries, factor, share, first, earlier=None, strips_per_step=16, rows_per_step=160):
    strips, rows, chans = gathered.shape
    width = queries.shape[1]
    row_steps = rows // rows_per_step
    grid = (row_steps, strips // strips_per_step)
    in_specs = [
        pl.BlockSpec((strips_per_step, rows_per_step, chans), lambda i, j: (j, i, 0)),
        pl.BlockSpec((chans, width), lambda i, j: (0, 0)),
    ]
    operands = [gathered, queries]
    aliases = {}
    if earlier is not None:
        in_specs.append(pl.BlockSpec(memory_space=pl.ANY))
        operands.append(earlier)
        aliases = {2: 0}
    offset = first // rows_per_step
    return pl.pallas_call(
        functools.partial(correlate_kernel, factor),
        out_shape=jax.ShapeDtypeStruct((share, strips, width), jnp.bfloat16),
        grid=grid,
        in_specs=in_specs,
        out_specs=pl.BlockSpec((rows_per_step, strips_per_step, width), lambda i, j: (i + offset, j, 0)),
        input_output_aliases=aliases,
        cost_estimate=pl.CostEstimate(
            flops=2 * strips * rows * chans * width,
            bytes_accessed=2 * (strips * rows * chans + width * chans + strips * rows * width),
            transcendentals=0,
        ),
    )(*operands)


def local(frame_one, frame_two):
    queries = lax.all_gather(frame_one, "chan", axis=1, tiled=True)
    channels = queries.shape[1]
    factor = 1.0 / float(channels) ** 0.5
    pooled = pool_strip(frame_two)
    groups = lax.axis_size("chan")
    share = pooled.shape[0] // groups
    slices = pooled.shape[1]
    blocks = jnp.transpose(pooled.reshape(groups, share, slices), (0, 2, 1))
    traded = trade(blocks)
    traded = jnp.transpose(traded, (2, 0, 1)).reshape(share, channels)
    chunks = 2
    chunk_rows = -(-share // (160 * chunks)) * 160
    traded = jnp.pad(traded, ((0, chunk_rows * chunks - share), (0, 0)))
    weights = queries.T
    values = None
    for c in range(chunks):
        piece = traded[c * chunk_rows:(c + 1) * chunk_rows]
        gathered = lax.all_gather(piece, "rows", axis=0, tiled=False)
        values = correlate(gathered, weights, factor, share, c * chunk_rows, values)
    return jnp.transpose(values, (1, 0, 2))


def solution(mesh):
    in_specs = (P("rows", "chan"), P("rows", None, "chan"))
    out_specs = P(None, "chan", "rows")
    return jax.shard_map(local, mesh=mesh, in_specs=in_specs, out_specs=out_specs, check_vma=False)
```

```python
import functools

import jax
import jax.numpy as jnp
from jax import lax
from jax.experimental import pallas as pl
from jax.experimental.pallas import tpu as pltpu
from jax.sharding import PartitionSpec as P

MESH_ID = pl.DeviceIdType.MESH


def pool_strip(strip):
    full = strip.astype(jnp.float32)
    rows_n, cols_n, chans = full.shape
    level_one = full.reshape(rows_n // 2, 2, cols_n // 2, 2, chans).mean(axis=(1, 3))
    level_two = level_one.reshape(rows_n // 4, 2, cols_n // 4, 2, chans).mean(axis=(1, 3))
    joined = jnp.concatenate(
        [full.reshape(-1, chans), level_one.reshape(-1, chans), level_two.reshape(-1, chans)],
        axis=0,
    )
    return joined.astype(jnp.bfloat16)


def trade_kernel(n, x_ref, o_ref, buf, send_sem, recv_sem):
    me = lax.axis_index("chan")
    row = lax.axis_index("rows")
    barrier = pltpu.get_barrier_semaphore()
    for k in range(1, n):
        peer = lax.rem(me + k, n)
        pl.semaphore_signal(barrier, inc=1, device_id=(row, peer), device_id_type=MESH_ID)
    pl.semaphore_wait(barrier, n - 1)
    sends = []
    for k in range(1, n):
        peer = lax.rem(me + k, n)
        copy = pltpu.make_async_remote_copy(
            src_ref=x_ref.at[peer],
            dst_ref=buf.at[me],
            send_sem=send_sem.at[k],
            recv_sem=recv_sem.at[k],
            device_id=(row, peer),
            device_id_type=MESH_ID,
        )
        copy.start()
        sends.append(copy)
    o_ref[me] = x_ref[me]
    for k in range(1, n):
        source = lax.rem(me + n - k, n)
        arrival = pltpu.make_async_remote_copy(
            src_ref=x_ref.at[me],
            dst_ref=buf.at[source],
            send_sem=send_sem.at[k],
            recv_sem=recv_sem.at[k],
            device_id=(row, source),
            device_id_type=MESH_ID,
        )
        arrival.wait_recv()
        o_ref[source] = buf[source]
    for copy in sends:
        copy.wait_send()


def trade(blocks):
    n = blocks.shape[0]
    return pl.pallas_call(
        functools.partial(trade_kernel, n),
        out_shape=jax.ShapeDtypeStruct(blocks.shape, blocks.dtype),
        in_specs=[pl.BlockSpec(memory_space=pltpu.VMEM)],
        out_specs=pl.BlockSpec(memory_space=pltpu.VMEM),
        scratch_shapes=[
            pltpu.VMEM(blocks.shape, blocks.dtype),
            pltpu.SemaphoreType.DMA((n,)),
            pltpu.SemaphoreType.DMA((n,)),
        ],
        compiler_params=pltpu.CompilerParams(collective_id=0, has_side_effects=True),
    )(blocks)


def gather_kernel(zn, piece_ref, out_ref, send_sem, recv_sem, local_sem):
    row = lax.axis_index("rows")
    col = lax.axis_index("chan")
    b = row % 2
    ylo = (row // 2) % 2
    z = row // 4
    m = ylo * 2 + b
    other = 1 - ylo

    def device(zz, yy, cc):
        return (((zz % zn) * 2 + yy) * 2 + cc, col)

    partner = device(z, ylo, 1 - b)
    ups = device(z + 1, ylo, b)
    downs = device(z + zn - 1, ylo, b)
    side = [device(z, other, c) for c in range(2)]

    barrier = pltpu.get_barrier_semaphore()
    for peer in [partner, ups, downs] + side:
        pl.semaphore_signal(barrier, inc=1, device_id=peer, device_id_type=MESH_ID)
    pl.semaphore_wait(barrier, 5)

    def remote(src, dst, idx, peer, arrival=None):
        arrival = idx if arrival is None else arrival
        return pltpu.make_async_remote_copy(
            src_ref=src, dst_ref=dst, send_sem=send_sem.at[idx], recv_sem=recv_sem.at[arrival],
            device_id=peer, device_id_type=MESH_ID,
        )

    started = []

    def send(src, dst, idx, peer, arrival=None):
        copy = remote(src, dst, idx, peer, arrival)
        copy.start()
        started.append(copy)

    def arrive(dst, idx):
        remote(dst, dst, idx, partner).wait_recv()

    own = []
    for h in range(2):
        copy = pltpu.make_async_copy(piece_ref.at[h], out_ref.at[h, z, m], local_sem.at[h])
        copy.start()
        own.append(copy)
    for h in range(2):
        send(piece_ref.at[h], out_ref.at[h, z, m], h, partner)
    for c in range(2):
        send(piece_ref.at[c], out_ref.at[c, z, m], 2 + c, side[c], 4 + b)
    for copy in own:
        copy.wait()
    arrive(out_ref.at[b, z, ylo * 2 + 1 - b], b)
    arrive(out_ref.at[1 - b, z, ylo * 2 + 1 - b], 1 - b)
    side_slots = pl.ds(other * 2, 2)
    for c in range(2):
        arrive(out_ref.at[b, z, other * 2 + c], 4 + c)
    send(out_ref.at[b, z, side_slots], out_ref.at[b, z, side_slots], 14, partner)

    steps = zn // 2
    for t in range(1, steps + 1):
        up_block = (z - (t - 1) + zn) % zn
        down_block = (z + (t - 1)) % zn
        if t < steps:
            up_src = out_ref.at[b, up_block]
            down_src = out_ref.at[b, down_block]
        else:
            up_src = out_ref.at[b, up_block, pl.ds(0, 2)]
            down_src = out_ref.at[b, down_block, pl.ds(2, 2)]
        send(up_src, up_src, 6 + (t - 1), ups)
        send(down_src, down_src, 10 + (t - 1), downs)
        got_up = (z - t + zn) % zn
        got_down = (z + t) % zn
        if t < steps:
            up_dst = out_ref.at[b, got_up]
            down_dst = out_ref.at[b, got_down]
        else:
            up_dst = out_ref.at[b, got_up, pl.ds(0, 2)]
            down_dst = out_ref.at[b, got_down, pl.ds(2, 2)]
        arrive(up_dst, 6 + (t - 1))
        send(up_dst, up_dst, 15 + (t - 1), partner)
        arrive(down_dst, 10 + (t - 1))
        send(down_dst, down_dst, 19 + (t - 1), partner)

    arrive(out_ref.at[1 - b, z, side_slots], 14)
    for t in range(1, steps + 1):
        got_up = (z - t + zn) % zn
        got_down = (z + t) % zn
        if t < steps:
            up_dst = out_ref.at[1 - b, got_up]
            down_dst = out_ref.at[1 - b, got_down]
        else:
            up_dst = out_ref.at[1 - b, got_up, pl.ds(0, 2)]
            down_dst = out_ref.at[1 - b, got_down, pl.ds(2, 2)]
        arrive(up_dst, 15 + (t - 1))
        arrive(down_dst, 19 + (t - 1))
    for copy in started:
        copy.wait_send()


def gather(piece, strips):
    halves, rows, chans = piece.shape
    zn = strips // 4
    sems = 23
    out = pl.pallas_call(
        functools.partial(gather_kernel, zn),
        out_shape=jax.ShapeDtypeStruct((halves, zn, 4, rows, chans), piece.dtype),
        in_specs=[pl.BlockSpec(memory_space=pl.ANY)],
        out_specs=pl.BlockSpec(memory_space=pl.ANY),
        scratch_shapes=[
            pltpu.SemaphoreType.DMA((sems,)),
            pltpu.SemaphoreType.DMA((sems,)),
            pltpu.SemaphoreType.DMA((2,)),
        ],
        compiler_params=pltpu.CompilerParams(collective_id=1, has_side_effects=True),
    )(piece)
    return out.reshape(halves, strips, rows, chans)


def correlate_kernel(factor, x_ref, f_ref, o_ref):
    for s in range(x_ref.shape[0]):
        acc = jnp.dot(x_ref[s], f_ref[...], preferred_element_type=jnp.float32)
        o_ref[:, s, :] = (acc * factor).astype(o_ref.dtype)


def correlate(gathered, queries, factor, share, strips_per_step=16, rows_per_step=160):
    halves, strips, half_rows, chans = gathered.shape
    width = queries.shape[1]
    per_half = half_rows // rows_per_step
    grid = (pl.cdiv(share, rows_per_step), strips // strips_per_step)
    return pl.pallas_call(
        functools.partial(correlate_kernel, factor),
        out_shape=jax.ShapeDtypeStruct((share, strips, width), jnp.bfloat16),
        grid=grid,
        in_specs=[
            pl.BlockSpec(
                (None, strips_per_step, rows_per_step, chans),
                lambda i, j: (i // per_half, j, i % per_half, 0),
            ),
            pl.BlockSpec((chans, width), lambda i, j: (0, 0)),
        ],
        out_specs=pl.BlockSpec((rows_per_step, strips_per_step, width), lambda i, j: (i, j, 0)),
        cost_estimate=pl.CostEstimate(
            flops=2 * strips * share * chans * width,
            bytes_accessed=2 * (strips * share * chans + width * chans + strips * share * width),
            transcendentals=0,
        ),
    )(gathered, queries)


def local(frame_one, frame_two):
    queries = lax.all_gather(frame_one, "chan", axis=1, tiled=True)
    channels = queries.shape[1]
    factor = 1.0 / float(channels) ** 0.5
    pooled = pool_strip(frame_two)
    groups = lax.axis_size("chan")
    strips = lax.axis_size("rows")
    share = pooled.shape[0] // groups
    slices = pooled.shape[1]
    blocks = jnp.transpose(pooled.reshape(groups, share, slices), (0, 2, 1))
    traded = trade(blocks)
    traded = jnp.transpose(traded, (2, 0, 1)).reshape(share, channels)
    padded = -(-share // 320) * 320
    traded = jnp.pad(traded, ((0, padded - share), (0, 0)))
    gathered = gather(traded.reshape(2, padded // 2, channels), strips)
    values = correlate(gathered, queries.T, factor, share)
    return jnp.transpose(values, (1, 0, 2))


def solution(mesh):
    in_specs = (P("rows", "chan"), P("rows", None, "chan"))
    out_specs = P(None, "chan", "rows")
    return jax.shard_map(local, mesh=mesh, in_specs=in_specs, out_specs=out_specs, check_vma=False)
```

```python
import functools

import jax
import jax.numpy as jnp
from jax import lax
from jax.experimental import pallas as pl
from jax.experimental.pallas import tpu as pltpu
from jax.sharding import PartitionSpec as P

MESH_ID = pl.DeviceIdType.MESH


def pool_strip(strip):
    full = strip.astype(jnp.float32)
    rows_n, cols_n, chans = full.shape
    level_one = full.reshape(rows_n // 2, 2, cols_n // 2, 2, chans).mean(axis=(1, 3))
    level_two = level_one.reshape(rows_n // 4, 2, cols_n // 4, 2, chans).mean(axis=(1, 3))
    joined = jnp.concatenate(
        [full.reshape(-1, chans), level_one.reshape(-1, chans), level_two.reshape(-1, chans)],
        axis=0,
    )
    return joined.astype(jnp.bfloat16)


def trade_kernel(n, x_ref, f_ref, o_ref, g_ref, buf, fbuf, send_sem, recv_sem, fsend_sem, frecv_sem):
    me = lax.axis_index("chan")
    row = lax.axis_index("rows")
    barrier = pltpu.get_barrier_semaphore()
    for k in range(1, n):
        peer = lax.rem(me + k, n)
        pl.semaphore_signal(barrier, inc=1, device_id=(row, peer), device_id_type=MESH_ID)
    pl.semaphore_wait(barrier, n - 1)
    sends = []
    for k in range(1, n):
        peer = lax.rem(me + k, n)
        for src, dst, ssem, rsem in ((x_ref.at[peer], buf.at[me], send_sem, recv_sem), (f_ref, fbuf.at[me], fsend_sem, frecv_sem)):
            copy = pltpu.make_async_remote_copy(
                src_ref=src,
                dst_ref=dst,
                send_sem=ssem.at[k],
                recv_sem=rsem.at[k],
                device_id=(row, peer),
                device_id_type=MESH_ID,
            )
            copy.start()
            sends.append(copy)
    o_ref[me] = x_ref[me]
    g_ref[me] = f_ref[...]
    for k in range(1, n):
        source = lax.rem(me + n - k, n)
        for src, dst, ssem, rsem, out in ((x_ref.at[me], buf.at[source], send_sem, recv_sem, o_ref), (f_ref, fbuf.at[source], fsend_sem, frecv_sem, g_ref)):
            arrival = pltpu.make_async_remote_copy(
                src_ref=src,
                dst_ref=dst,
                send_sem=ssem.at[k],
                recv_sem=rsem.at[k],
                device_id=(row, source),
                device_id_type=MESH_ID,
            )
            arrival.wait_recv()
            out[source] = dst[...]
    for copy in sends:
        copy.wait_send()


def trade(blocks, piece):
    n = blocks.shape[0]
    gathered = (n,) + piece.shape
    return pl.pallas_call(
        functools.partial(trade_kernel, n),
        out_shape=(
            jax.ShapeDtypeStruct(blocks.shape, blocks.dtype),
            jax.ShapeDtypeStruct(gathered, piece.dtype),
        ),
        in_specs=[pl.BlockSpec(memory_space=pltpu.VMEM)] * 2,
        out_specs=(pl.BlockSpec(memory_space=pltpu.VMEM),) * 2,
        scratch_shapes=[
            pltpu.VMEM(blocks.shape, blocks.dtype),
            pltpu.VMEM(gathered, piece.dtype),
            pltpu.SemaphoreType.DMA((n,)),
            pltpu.SemaphoreType.DMA((n,)),
            pltpu.SemaphoreType.DMA((n,)),
            pltpu.SemaphoreType.DMA((n,)),
        ],
        compiler_params=pltpu.CompilerParams(collective_id=0, has_side_effects=True),
    )(blocks, piece)


def gather_kernel(zn, piece_ref, out_ref, send_sem, recv_sem, local_sem):
    row = lax.axis_index("rows")
    col = lax.axis_index("chan")
    b = row % 2
    ylo = (row // 2) % 2
    z = row // 4
    m = ylo * 2 + b
    other = 1 - ylo

    def device(zz, yy, cc):
        return (((zz % zn) * 2 + yy) * 2 + cc, col)

    partner = device(z, ylo, 1 - b)
    ups = device(z + 1, ylo, b)
    downs = device(z + zn - 1, ylo, b)
    side = [device(z, other, c) for c in range(2)]

    barrier = pltpu.get_barrier_semaphore()
    for peer in [partner, ups, downs] + side:
        pl.semaphore_signal(barrier, inc=1, device_id=peer, device_id_type=MESH_ID)
    pl.semaphore_wait(barrier, 5)

    def remote(src, dst, idx, peer, arrival=None):
        arrival = idx if arrival is None else arrival
        return pltpu.make_async_remote_copy(
            src_ref=src, dst_ref=dst, send_sem=send_sem.at[idx], recv_sem=recv_sem.at[arrival],
            device_id=peer, device_id_type=MESH_ID,
        )

    started = []

    def send(src, dst, idx, peer, arrival=None):
        copy = remote(src, dst, idx, peer, arrival)
        copy.start()
        started.append(copy)

    def arrive(dst, idx):
        remote(dst, dst, idx, partner).wait_recv()

    own = []
    for h in range(2):
        copy = pltpu.make_async_copy(piece_ref.at[h], out_ref.at[h, z, m], local_sem.at[h])
        copy.start()
        own.append(copy)
    for h in range(2):
        send(piece_ref.at[h], out_ref.at[h, z, m], h, partner)
    for c in range(2):
        send(piece_ref.at[c], out_ref.at[c, z, m], 2 + c, side[c], 4 + b)
    for copy in own:
        copy.wait()
    arrive(out_ref.at[b, z, ylo * 2 + 1 - b], b)
    arrive(out_ref.at[1 - b, z, ylo * 2 + 1 - b], 1 - b)
    side_slots = pl.ds(other * 2, 2)
    for c in range(2):
        arrive(out_ref.at[b, z, other * 2 + c], 4 + c)
    send(out_ref.at[b, z, side_slots], out_ref.at[b, z, side_slots], 14, partner)

    steps = zn // 2
    for t in range(1, steps + 1):
        up_block = (z - (t - 1) + zn) % zn
        down_block = (z + (t - 1)) % zn
        if t < steps:
            up_src = out_ref.at[b, up_block]
            down_src = out_ref.at[b, down_block]
        else:
            up_src = out_ref.at[b, up_block, pl.ds(0, 2)]
            down_src = out_ref.at[b, down_block, pl.ds(2, 2)]
        send(up_src, up_src, 6 + (t - 1), ups)
        send(down_src, down_src, 10 + (t - 1), downs)
        got_up = (z - t + zn) % zn
        got_down = (z + t) % zn
        if t < steps:
            up_dst = out_ref.at[b, got_up]
            down_dst = out_ref.at[b, got_down]
        else:
            up_dst = out_ref.at[b, got_up, pl.ds(0, 2)]
            down_dst = out_ref.at[b, got_down, pl.ds(2, 2)]
        arrive(up_dst, 6 + (t - 1))
        send(up_dst, up_dst, 15 + (t - 1), partner)
        arrive(down_dst, 10 + (t - 1))
        send(down_dst, down_dst, 19 + (t - 1), partner)

    arrive(out_ref.at[1 - b, z, side_slots], 14)
    for t in range(1, steps + 1):
        got_up = (z - t + zn) % zn
        got_down = (z + t) % zn
        if t < steps:
            up_dst = out_ref.at[1 - b, got_up]
            down_dst = out_ref.at[1 - b, got_down]
        else:
            up_dst = out_ref.at[1 - b, got_up, pl.ds(0, 2)]
            down_dst = out_ref.at[1 - b, got_down, pl.ds(2, 2)]
        arrive(up_dst, 15 + (t - 1))
        arrive(down_dst, 19 + (t - 1))
    for copy in started:
        copy.wait_send()


def gather(piece, strips):
    halves, rows, chans = piece.shape
    zn = strips // 4
    sems = 23
    out = pl.pallas_call(
        functools.partial(gather_kernel, zn),
        out_shape=jax.ShapeDtypeStruct((halves, zn, 4, rows, chans), piece.dtype),
        in_specs=[pl.BlockSpec(memory_space=pl.ANY)],
        out_specs=pl.BlockSpec(memory_space=pl.ANY),
        scratch_shapes=[
            pltpu.SemaphoreType.DMA((sems,)),
            pltpu.SemaphoreType.DMA((sems,)),
            pltpu.SemaphoreType.DMA((2,)),
        ],
        compiler_params=pltpu.CompilerParams(collective_id=1, has_side_effects=True),
    )(piece)
    return out.reshape(halves, strips, rows, chans)


def correlate_kernel(factor, x_ref, f_ref, o_ref):
    for s in range(x_ref.shape[0]):
        acc = jnp.dot(x_ref[s], f_ref[...], preferred_element_type=jnp.float32)
        o_ref[:, s, :] = (acc * factor).astype(o_ref.dtype)


def correlate(gathered, queries, factor, share, strips_per_step=16, rows_per_step=160):
    halves, strips, half_rows, chans = gathered.shape
    width = queries.shape[1]
    per_half = half_rows // rows_per_step
    grid = (pl.cdiv(share, rows_per_step), strips // strips_per_step)
    return pl.pallas_call(
        functools.partial(correlate_kernel, factor),
        out_shape=jax.ShapeDtypeStruct((share, strips, width), jnp.bfloat16),
        grid=grid,
        in_specs=[
            pl.BlockSpec(
                (None, strips_per_step, rows_per_step, chans),
                lambda i, j: (i // per_half, j, i % per_half, 0),
            ),
            pl.BlockSpec((chans, width), lambda i, j: (0, 0)),
        ],
        out_specs=pl.BlockSpec((rows_per_step, strips_per_step, width), lambda i, j: (i, j, 0)),
        cost_estimate=pl.CostEstimate(
            flops=2 * strips * share * chans * width,
            bytes_accessed=2 * (strips * share * chans + width * chans + strips * share * width),
            transcendentals=0,
        ),
    )(gathered, queries)


def local(frame_one, frame_two):
    pooled = pool_strip(frame_two)
    groups = lax.axis_size("chan")
    channels = groups * frame_one.shape[1]
    factor = 1.0 / float(channels) ** 0.5
    strips = lax.axis_size("rows")
    share = pooled.shape[0] // groups
    slices = pooled.shape[1]
    blocks = jnp.transpose(pooled.reshape(groups, share, slices), (0, 2, 1))
    traded, pieces = trade(blocks, frame_one.T)
    weights = pieces.reshape(channels, frame_one.shape[0])
    traded = jnp.transpose(traded, (2, 0, 1)).reshape(share, channels)
    padded = -(-share // 320) * 320
    traded = jnp.pad(traded, ((0, padded - share), (0, 0)))
    gathered = gather(traded.reshape(2, padded // 2, channels), strips)
    values = correlate(gathered, weights, factor, share)
    return jnp.transpose(values, (1, 0, 2))


def solution(mesh):
    in_specs = (P("rows", "chan"), P("rows", None, "chan"))
    out_specs = P(None, "chan", "rows")
    return jax.shard_map(local, mesh=mesh, in_specs=in_specs, out_specs=out_specs, check_vma=False)
```

```python
import functools

import jax
import jax.numpy as jnp
from jax import lax
from jax.experimental import pallas as pl
from jax.experimental.pallas import tpu as pltpu
from jax.sharding import PartitionSpec as P

MESH_ID = pl.DeviceIdType.MESH


def pool_strip(strip):
    full = strip.astype(jnp.float32)
    rows_n, cols_n, chans = full.shape
    level_one = full.reshape(rows_n // 2, 2, cols_n // 2, 2, chans).mean(axis=(1, 3))
    level_two = level_one.reshape(rows_n // 4, 2, cols_n // 4, 2, chans).mean(axis=(1, 3))
    joined = jnp.concatenate(
        [full.reshape(-1, chans), level_one.reshape(-1, chans), level_two.reshape(-1, chans)],
        axis=0,
    )
    return joined.astype(jnp.bfloat16)


def trade_kernel(n, x_ref, f_ref, o_ref, g_ref, buf, fbuf, send_sem, recv_sem, fsend_sem, frecv_sem):
    me = lax.axis_index("chan")
    row = lax.axis_index("rows")
    barrier = pltpu.get_barrier_semaphore()
    for k in range(1, n):
        peer = lax.rem(me + k, n)
        pl.semaphore_signal(barrier, inc=1, device_id=(row, peer), device_id_type=MESH_ID)
    pl.semaphore_wait(barrier, n - 1)
    sends = []
    for k in range(1, n):
        peer = lax.rem(me + k, n)
        for src, dst, ssem, rsem in ((x_ref.at[peer], buf.at[me], send_sem, recv_sem), (f_ref, fbuf.at[me], fsend_sem, frecv_sem)):
            copy = pltpu.make_async_remote_copy(
                src_ref=src,
                dst_ref=dst,
                send_sem=ssem.at[k],
                recv_sem=rsem.at[k],
                device_id=(row, peer),
                device_id_type=MESH_ID,
            )
            copy.start()
            sends.append(copy)
    o_ref[me] = x_ref[me]
    g_ref[me] = f_ref[...]
    for k in range(1, n):
        source = lax.rem(me + n - k, n)
        for src, dst, ssem, rsem, out in ((x_ref.at[me], buf.at[source], send_sem, recv_sem, o_ref), (f_ref, fbuf.at[source], fsend_sem, frecv_sem, g_ref)):
            arrival = pltpu.make_async_remote_copy(
                src_ref=src,
                dst_ref=dst,
                send_sem=ssem.at[k],
                recv_sem=rsem.at[k],
                device_id=(row, source),
                device_id_type=MESH_ID,
            )
            arrival.wait_recv()
            out[source] = dst[...]
    for copy in sends:
        copy.wait_send()


def trade(blocks, piece):
    n = blocks.shape[0]
    gathered = (n,) + piece.shape
    return pl.pallas_call(
        functools.partial(trade_kernel, n),
        out_shape=(
            jax.ShapeDtypeStruct(blocks.shape, blocks.dtype),
            jax.ShapeDtypeStruct(gathered, piece.dtype),
        ),
        in_specs=[pl.BlockSpec(memory_space=pltpu.VMEM)] * 2,
        out_specs=(pl.BlockSpec(memory_space=pltpu.VMEM),) * 2,
        scratch_shapes=[
            pltpu.VMEM(blocks.shape, blocks.dtype),
            pltpu.VMEM(gathered, piece.dtype),
            pltpu.SemaphoreType.DMA((n,)),
            pltpu.SemaphoreType.DMA((n,)),
            pltpu.SemaphoreType.DMA((n,)),
            pltpu.SemaphoreType.DMA((n,)),
        ],
        compiler_params=pltpu.CompilerParams(collective_id=0, has_side_effects=True),
    )(blocks, piece)


def gather_kernel(zn, piece_ref, out_ref, send_sem, recv_sem, local_sem):
    row = lax.axis_index("rows")
    col = lax.axis_index("chan")
    b = row % 2
    ylo = (row // 2) % 2
    z = row // 4
    m = ylo * 2 + b
    other = 1 - ylo

    def device(zz, yy, cc):
        return (((zz % zn) * 2 + yy) * 2 + cc, col)

    partner = device(z, ylo, 1 - b)
    ups = device(z + 1, ylo, b)
    downs = device(z + zn - 1, ylo, b)
    side = [device(z, other, c) for c in range(2)]

    barrier = pltpu.get_barrier_semaphore()
    for peer in [partner, ups, downs] + side:
        pl.semaphore_signal(barrier, inc=1, device_id=peer, device_id_type=MESH_ID)
    pl.semaphore_wait(barrier, 5)

    def remote(src, dst, idx, peer, arrival=None):
        arrival = idx if arrival is None else arrival
        return pltpu.make_async_remote_copy(
            src_ref=src, dst_ref=dst, send_sem=send_sem.at[idx], recv_sem=recv_sem.at[arrival],
            device_id=peer, device_id_type=MESH_ID,
        )

    started = []

    def send(src, dst, idx, peer, arrival=None):
        copy = remote(src, dst, idx, peer, arrival)
        copy.start()
        started.append(copy)

    def arrive(dst, idx):
        remote(dst, dst, idx, partner).wait_recv()

    own = []
    for h in range(2):
        copy = pltpu.make_async_copy(piece_ref.at[h], out_ref.at[h, z, m], local_sem.at[h])
        copy.start()
        own.append(copy)
    for h in range(2):
        send(piece_ref.at[h], out_ref.at[h, z, m], h, partner)
    for c in range(2):
        send(piece_ref.at[c], out_ref.at[c, z, m], 2 + c, side[c], 4 + b)
    for copy in own:
        copy.wait()
    arrive(out_ref.at[b, z, ylo * 2 + 1 - b], b)
    arrive(out_ref.at[1 - b, z, ylo * 2 + 1 - b], 1 - b)
    side_slots = pl.ds(other * 2, 2)
    for c in range(2):
        arrive(out_ref.at[b, z, other * 2 + c], 4 + c)
    send(out_ref.at[b, z, side_slots], out_ref.at[b, z, side_slots], 22, partner)

    steps = zn // 2
    rows = piece_ref.shape[1]
    carried = pl.ds(ylo, 3)
    lent = 3 * ylo
    wanted = 3 * other
    up_rows = pl.ds(0, rows // 2)
    down_rows = pl.ds(rows // 2, rows // 2)
    ring_regions = []
    for t in range(1, steps + 1):
        up_block = (z - (t - 1) + zn) % zn
        down_block = (z + (t - 1)) % zn
        if t < steps:
            up_src = out_ref.at[b, up_block, carried]
            down_src = out_ref.at[b, down_block, carried]
        else:
            up_src = out_ref.at[b, up_block, carried, up_rows]
            down_src = out_ref.at[b, down_block, carried, down_rows]
        send(up_src, up_src, 6 + (t - 1), ups)
        send(down_src, down_src, 10 + (t - 1), downs)
        got_up = (z - t + zn) % zn
        got_down = (z + t) % zn
        picks = [(got_up, 6, 14, 23, 31, up_rows), (got_down, 10, 18, 27, 35, down_rows)]
        for block, ring_idx, lend_idx, fwd_idx, fwd_lent_idx, part in picks:
            if t < steps:
                dst = out_ref.at[b, block, carried]
                lend = out_ref.at[b, block, lent]
            else:
                dst = out_ref.at[b, block, carried, part]
                lend = out_ref.at[b, block, lent, part]
            arrive(dst, ring_idx + (t - 1))
            send(lend, lend, lend_idx + (t - 1), device(z, other, b))
            send(dst, dst, fwd_idx + (t - 1), partner)
            ring_regions.append((block, part, ring_idx, lend_idx, fwd_idx, fwd_lent_idx, t))
    for block, part, ring_idx, lend_idx, fwd_idx, fwd_lent_idx, t in ring_regions:
        if t < steps:
            got = out_ref.at[b, block, wanted]
        else:
            got = out_ref.at[b, block, wanted, part]
        arrive(got, lend_idx + (t - 1))
        send(got, got, fwd_lent_idx + (t - 1), partner)

    arrive(out_ref.at[1 - b, z, side_slots], 22)
    for block, part, ring_idx, lend_idx, fwd_idx, fwd_lent_idx, t in ring_regions:
        if t < steps:
            dst = out_ref.at[1 - b, block, carried]
            got = out_ref.at[1 - b, block, wanted]
        else:
            dst = out_ref.at[1 - b, block, carried, part]
            got = out_ref.at[1 - b, block, wanted, part]
        arrive(dst, fwd_idx + (t - 1))
        arrive(got, fwd_lent_idx + (t - 1))
    for copy in started:
        copy.wait_send()


def gather(piece, strips):
    halves, rows, chans = piece.shape
    zn = strips // 4
    sems = 39
    out = pl.pallas_call(
        functools.partial(gather_kernel, zn),
        out_shape=jax.ShapeDtypeStruct((halves, zn, 4, rows, chans), piece.dtype),
        in_specs=[pl.BlockSpec(memory_space=pl.ANY)],
        out_specs=pl.BlockSpec(memory_space=pl.ANY),
        scratch_shapes=[
            pltpu.SemaphoreType.DMA((sems,)),
            pltpu.SemaphoreType.DMA((sems,)),
            pltpu.SemaphoreType.DMA((2,)),
        ],
        compiler_params=pltpu.CompilerParams(collective_id=1, has_side_effects=True),
    )(piece)
    return out.reshape(halves, strips, rows, chans)


def correlate_kernel(factor, x_ref, f_ref, o_ref):
    for s in range(x_ref.shape[0]):
        acc = jnp.dot(x_ref[s], f_ref[...], preferred_element_type=jnp.float32)
        o_ref[:, s, :] = (acc * factor).astype(o_ref.dtype)


def correlate(gathered, queries, factor, share, strips_per_step=16, rows_per_step=160):
    halves, strips, half_rows, chans = gathered.shape
    width = queries.shape[1]
    per_half = half_rows // rows_per_step
    grid = (pl.cdiv(share, rows_per_step), strips // strips_per_step)
    return pl.pallas_call(
        functools.partial(correlate_kernel, factor),
        out_shape=jax.ShapeDtypeStruct((share, strips, width), jnp.bfloat16),
        grid=grid,
        in_specs=[
            pl.BlockSpec(
                (None, strips_per_step, rows_per_step, chans),
                lambda i, j: (i // per_half, j, i % per_half, 0),
            ),
            pl.BlockSpec((chans, width), lambda i, j: (0, 0)),
        ],
        out_specs=pl.BlockSpec((rows_per_step, strips_per_step, width), lambda i, j: (i, j, 0)),
        cost_estimate=pl.CostEstimate(
            flops=2 * strips * share * chans * width,
            bytes_accessed=2 * (strips * share * chans + width * chans + strips * share * width),
            transcendentals=0,
        ),
    )(gathered, queries)


def local(frame_one, frame_two):
    pooled = pool_strip(frame_two)
    groups = lax.axis_size("chan")
    channels = groups * frame_one.shape[1]
    factor = 1.0 / float(channels) ** 0.5
    strips = lax.axis_size("rows")
    share = pooled.shape[0] // groups
    slices = pooled.shape[1]
    blocks = jnp.transpose(pooled.reshape(groups, share, slices), (0, 2, 1))
    traded, pieces = trade(blocks, frame_one.T)
    weights = pieces.reshape(channels, frame_one.shape[0])
    traded = jnp.transpose(traded, (2, 0, 1)).reshape(share, channels)
    padded = -(-share // 320) * 320
    traded = jnp.pad(traded, ((0, padded - share), (0, 0)))
    gathered = gather(traded.reshape(2, padded // 2, channels), strips)
    values = correlate(gathered, weights, factor, share)
    return jnp.transpose(values, (1, 0, 2))


def solution(mesh):
    in_specs = (P("rows", "chan"), P("rows", None, "chan"))
    out_specs = P(None, "chan", "rows")
    return jax.shard_map(local, mesh=mesh, in_specs=in_specs, out_specs=out_specs, check_vma=False)
```

```python
import functools

import jax
import jax.numpy as jnp
from jax import lax
from jax.experimental import pallas as pl
from jax.experimental.pallas import tpu as pltpu
from jax.sharding import PartitionSpec as P

MESH_ID = pl.DeviceIdType.MESH


def pool_strip(strip):
    full = strip.astype(jnp.float32)
    rows_n, cols_n, chans = full.shape
    level_one = full.reshape(rows_n // 2, 2, cols_n // 2, 2, chans).mean(axis=(1, 3))
    level_two = level_one.reshape(rows_n // 4, 2, cols_n // 4, 2, chans).mean(axis=(1, 3))
    joined = jnp.concatenate(
        [full.reshape(-1, chans), level_one.reshape(-1, chans), level_two.reshape(-1, chans)],
        axis=0,
    )
    return joined.astype(jnp.bfloat16)


def trade_kernel(n, x_ref, f_ref, o_ref, g_ref, buf, fbuf, send_sem, recv_sem, fsend_sem, frecv_sem):
    me = lax.axis_index("chan")
    row = lax.axis_index("rows")
    barrier = pltpu.get_barrier_semaphore()
    for k in range(1, n):
        peer = lax.rem(me + k, n)
        pl.semaphore_signal(barrier, inc=1, device_id=(row, peer), device_id_type=MESH_ID)
    pl.semaphore_wait(barrier, n - 1)
    sends = []
    for k in range(1, n):
        peer = lax.rem(me + k, n)
        for src, dst, ssem, rsem in ((x_ref.at[peer], buf.at[me], send_sem, recv_sem), (f_ref, fbuf.at[me], fsend_sem, frecv_sem)):
            copy = pltpu.make_async_remote_copy(
                src_ref=src,
                dst_ref=dst,
                send_sem=ssem.at[k],
                recv_sem=rsem.at[k],
                device_id=(row, peer),
                device_id_type=MESH_ID,
            )
            copy.start()
            sends.append(copy)
    o_ref[me] = x_ref[me]
    g_ref[me] = f_ref[...]
    for k in range(1, n):
        source = lax.rem(me + n - k, n)
        for src, dst, ssem, rsem, out in ((x_ref.at[me], buf.at[source], send_sem, recv_sem, o_ref), (f_ref, fbuf.at[source], fsend_sem, frecv_sem, g_ref)):
            arrival = pltpu.make_async_remote_copy(
                src_ref=src,
                dst_ref=dst,
                send_sem=ssem.at[k],
                recv_sem=rsem.at[k],
                device_id=(row, source),
                device_id_type=MESH_ID,
            )
            arrival.wait_recv()
            out[source] = dst[...]
    for copy in sends:
        copy.wait_send()


def trade(blocks, piece):
    n = blocks.shape[0]
    gathered = (n,) + piece.shape
    return pl.pallas_call(
        functools.partial(trade_kernel, n),
        out_shape=(
            jax.ShapeDtypeStruct(blocks.shape, blocks.dtype),
            jax.ShapeDtypeStruct(gathered, piece.dtype),
        ),
        in_specs=[pl.BlockSpec(memory_space=pltpu.VMEM)] * 2,
        out_specs=(pl.BlockSpec(memory_space=pltpu.VMEM),) * 2,
        scratch_shapes=[
            pltpu.VMEM(blocks.shape, blocks.dtype),
            pltpu.VMEM(gathered, piece.dtype),
            pltpu.SemaphoreType.DMA((n,)),
            pltpu.SemaphoreType.DMA((n,)),
            pltpu.SemaphoreType.DMA((n,)),
            pltpu.SemaphoreType.DMA((n,)),
        ],
        compiler_params=pltpu.CompilerParams(collective_id=0, has_side_effects=True),
    )(blocks, piece)


def gather_kernel(zn, piece_ref, out_ref, send_sem, recv_sem, local_sem):
    row = lax.axis_index("rows")
    col = lax.axis_index("chan")
    b = row % 2
    ylo = (row // 2) % 2
    z = row // 4
    m = ylo * 2 + b
    other = 1 - ylo

    def device(zz, yy, cc):
        return (((zz % zn) * 2 + yy) * 2 + cc, col)

    partner = device(z, ylo, 1 - b)
    ups = device(z + 1, ylo, b)
    downs = device(z + zn - 1, ylo, b)
    side = [device(z, other, c) for c in range(2)]

    barrier = pltpu.get_barrier_semaphore()
    for peer in [partner, ups, downs] + side:
        pl.semaphore_signal(barrier, inc=1, device_id=peer, device_id_type=MESH_ID)
    pl.semaphore_wait(barrier, 5)

    def remote(src, dst, idx, peer, arrival=None):
        arrival = idx if arrival is None else arrival
        return pltpu.make_async_remote_copy(
            src_ref=src, dst_ref=dst, send_sem=send_sem.at[idx], recv_sem=recv_sem.at[arrival],
            device_id=peer, device_id_type=MESH_ID,
        )

    started = []

    def send(src, dst, idx, peer, arrival=None):
        copy = remote(src, dst, idx, peer, arrival)
        copy.start()
        started.append(copy)

    def arrive(dst, idx):
        remote(dst, dst, idx, partner).wait_recv()

    own = []
    for h in range(2):
        copy = pltpu.make_async_copy(piece_ref.at[h], out_ref.at[h, z, m], local_sem.at[h])
        copy.start()
        own.append(copy)
    for h in range(2):
        send(piece_ref.at[h], out_ref.at[h, z, m], h, partner)
    for c in range(2):
        send(piece_ref.at[c], out_ref.at[c, z, m], 2 + c, side[c], 4 + b)
    for copy in own:
        copy.wait()
    arrive(out_ref.at[b, z, ylo * 2 + 1 - b], b)
    arrive(out_ref.at[1 - b, z, ylo * 2 + 1 - b], 1 - b)
    side_slots = pl.ds(other * 2, 2)
    for c in range(2):
        arrive(out_ref.at[b, z, other * 2 + c], 4 + c)
    send(out_ref.at[b, z, side_slots], out_ref.at[b, z, side_slots], 22, partner)

    steps = zn // 2
    rows = piece_ref.shape[1]
    carried = pl.ds(ylo, 3)
    lent = 3 * ylo
    wanted = 3 * other
    up_rows = pl.ds(0, rows // 2)
    down_rows = pl.ds(rows // 2, rows // 2)
    ring_regions = []
    for t in range(1, steps + 1):
        up_block = (z - (t - 1) + zn) % zn
        down_block = (z + (t - 1)) % zn
        if t < steps:
            up_src = out_ref.at[b, up_block, carried]
            down_src = out_ref.at[b, down_block, carried]
        else:
            up_src = out_ref.at[b, up_block, carried, up_rows]
            down_src = out_ref.at[b, down_block, carried, down_rows]
        send(up_src, up_src, 6 + (t - 1), ups)
        send(down_src, down_src, 10 + (t - 1), downs)
        got_up = (z - t + zn) % zn
        got_down = (z + t) % zn
        picks = [(got_up, 6, 14, 23, 31, up_rows), (got_down, 10, 18, 27, 35, down_rows)]
        for block, ring_idx, lend_idx, fwd_idx, fwd_lent_idx, part in picks:
            if t < steps:
                dst = out_ref.at[b, block, carried]
                lend = out_ref.at[b, block, lent]
            else:
                dst = out_ref.at[b, block, carried, part]
                lend = out_ref.at[b, block, lent, part]
            arrive(dst, ring_idx + (t - 1))
            send(lend, lend, lend_idx + (t - 1), device(z, other, b))
            send(dst, dst, fwd_idx + (t - 1), partner)
            ring_regions.append((block, part, ring_idx, lend_idx, fwd_idx, fwd_lent_idx, t))
    for block, part, ring_idx, lend_idx, fwd_idx, fwd_lent_idx, t in ring_regions:
        if t < steps:
            got = out_ref.at[b, block, wanted]
        else:
            got = out_ref.at[b, block, wanted, part]
        arrive(got, lend_idx + (t - 1))
        send(got, got, fwd_lent_idx + (t - 1), partner)

    arrive(out_ref.at[1 - b, z, side_slots], 22)
    for block, part, ring_idx, lend_idx, fwd_idx, fwd_lent_idx, t in ring_regions:
        if t < steps:
            dst = out_ref.at[1 - b, block, carried]
            got = out_ref.at[1 - b, block, wanted]
        else:
            dst = out_ref.at[1 - b, block, carried, part]
            got = out_ref.at[1 - b, block, wanted, part]
        arrive(dst, fwd_idx + (t - 1))
        arrive(got, fwd_lent_idx + (t - 1))
    for copy in started:
        copy.wait_send()


def gather(piece, strips):
    halves, rows, chans = piece.shape
    zn = strips // 4
    sems = 39
    out = pl.pallas_call(
        functools.partial(gather_kernel, zn),
        out_shape=jax.ShapeDtypeStruct((halves, zn, 4, rows, chans), piece.dtype),
        in_specs=[pl.BlockSpec(memory_space=pl.ANY)],
        out_specs=pl.BlockSpec(memory_space=pl.ANY),
        scratch_shapes=[
            pltpu.SemaphoreType.DMA((sems,)),
            pltpu.SemaphoreType.DMA((sems,)),
            pltpu.SemaphoreType.DMA((2,)),
        ],
        compiler_params=pltpu.CompilerParams(collective_id=1, has_side_effects=True),
    )(piece)
    return out.reshape(halves, strips, rows, chans)


def correlate_kernel(factor, x_ref, f_ref, o_ref, acc_ref):
    for s in range(x_ref.shape[0]):
        acc_ref[:, s, :] = jnp.dot(x_ref[s], f_ref[...], preferred_element_type=jnp.float32)
    o_ref[...] = (acc_ref[...] * factor).astype(o_ref.dtype)


def correlate(gathered, queries, factor, share, strips_per_step=16, rows_per_step=160):
    halves, strips, half_rows, chans = gathered.shape
    width = queries.shape[1]
    per_half = half_rows // rows_per_step
    grid = (pl.cdiv(share, rows_per_step), strips // strips_per_step)
    return pl.pallas_call(
        functools.partial(correlate_kernel, factor),
        out_shape=jax.ShapeDtypeStruct((share, strips, width), jnp.bfloat16),
        grid=grid,
        in_specs=[
            pl.BlockSpec(
                (None, strips_per_step, rows_per_step, chans),
                lambda i, j: (i // per_half, j, i % per_half, 0),
            ),
            pl.BlockSpec((chans, width), lambda i, j: (0, 0)),
        ],
        out_specs=pl.BlockSpec((rows_per_step, strips_per_step, width), lambda i, j: (i, j, 0)),
        scratch_shapes=[pltpu.VMEM((rows_per_step, strips_per_step, width), jnp.float32)],
        cost_estimate=pl.CostEstimate(
            flops=2 * strips * share * chans * width,
            bytes_accessed=2 * (strips * share * chans + width * chans + strips * share * width),
            transcendentals=0,
        ),
    )(gathered, queries)


def local(frame_one, frame_two):
    pooled = pool_strip(frame_two)
    groups = lax.axis_size("chan")
    channels = groups * frame_one.shape[1]
    factor = 1.0 / float(channels) ** 0.5
    strips = lax.axis_size("rows")
    share = pooled.shape[0] // groups
    slices = pooled.shape[1]
    blocks = jnp.transpose(pooled.reshape(groups, share, slices), (0, 2, 1))
    traded, pieces = trade(blocks, frame_one.T)
    weights = pieces.reshape(channels, frame_one.shape[0])
    traded = jnp.transpose(traded, (2, 0, 1)).reshape(share, channels)
    padded = -(-share // 320) * 320
    traded = jnp.pad(traded, ((0, padded - share), (0, 0)))
    gathered = gather(traded.reshape(2, padded // 2, channels), strips)
    values = correlate(gathered, weights, factor, share)
    return jnp.transpose(values, (1, 0, 2))


def solution(mesh):
    in_specs = (P("rows", "chan"), P("rows", None, "chan"))
    out_specs = P(None, "chan", "rows")
    return jax.shard_map(local, mesh=mesh, in_specs=in_specs, out_specs=out_specs, check_vma=False)
```

```python
import functools

import jax
import jax.numpy as jnp
from jax import lax
from jax.experimental import pallas as pl
from jax.experimental.pallas import tpu as pltpu
from jax.sharding import PartitionSpec as P

MESH_ID = pl.DeviceIdType.MESH


def pool_strip(strip):
    full = strip.astype(jnp.float32)
    rows_n, cols_n, chans = full.shape
    level_one = full.reshape(rows_n // 2, 2, cols_n // 2, 2, chans).mean(axis=(1, 3))
    level_two = level_one.reshape(rows_n // 4, 2, cols_n // 4, 2, chans).mean(axis=(1, 3))
    joined = jnp.concatenate(
        [full.reshape(-1, chans), level_one.reshape(-1, chans), level_two.reshape(-1, chans)],
        axis=0,
    )
    return joined.astype(jnp.bfloat16)


def trade_kernel(n, x_ref, f_ref, o_ref, g_ref, buf, fbuf, send_sem, recv_sem, fsend_sem, frecv_sem):
    me = lax.axis_index("chan")
    row = lax.axis_index("rows")
    barrier = pltpu.get_barrier_semaphore()
    for k in range(1, n):
        peer = lax.rem(me + k, n)
        pl.semaphore_signal(barrier, inc=1, device_id=(row, peer), device_id_type=MESH_ID)
    pl.semaphore_wait(barrier, n - 1)
    sends = []
    for k in range(1, n):
        peer = lax.rem(me + k, n)
        for src, dst, ssem, rsem in ((x_ref.at[peer], buf.at[me], send_sem, recv_sem), (f_ref, fbuf.at[me], fsend_sem, frecv_sem)):
            copy = pltpu.make_async_remote_copy(
                src_ref=src,
                dst_ref=dst,
                send_sem=ssem.at[k],
                recv_sem=rsem.at[k],
                device_id=(row, peer),
                device_id_type=MESH_ID,
            )
            copy.start()
            sends.append(copy)
    o_ref[me] = x_ref[me]
    g_ref[me] = f_ref[...]
    for k in range(1, n):
        source = lax.rem(me + n - k, n)
        for src, dst, ssem, rsem, out in ((x_ref.at[me], buf.at[source], send_sem, recv_sem, o_ref), (f_ref, fbuf.at[source], fsend_sem, frecv_sem, g_ref)):
            arrival = pltpu.make_async_remote_copy(
                src_ref=src,
                dst_ref=dst,
                send_sem=ssem.at[k],
                recv_sem=rsem.at[k],
                device_id=(row, source),
                device_id_type=MESH_ID,
            )
            arrival.wait_recv()
            out[source] = dst[...]
    for copy in sends:
        copy.wait_send()


def trade(blocks, piece):
    n = blocks.shape[0]
    gathered = (n,) + piece.shape
    return pl.pallas_call(
        functools.partial(trade_kernel, n),
        out_shape=(
            jax.ShapeDtypeStruct(blocks.shape, blocks.dtype),
            jax.ShapeDtypeStruct(gathered, piece.dtype),
        ),
        in_specs=[pl.BlockSpec(memory_space=pltpu.VMEM)] * 2,
        out_specs=(pl.BlockSpec(memory_space=pltpu.VMEM),) * 2,
        scratch_shapes=[
            pltpu.VMEM(blocks.shape, blocks.dtype),
            pltpu.VMEM(gathered, piece.dtype),
            pltpu.SemaphoreType.DMA((n,)),
            pltpu.SemaphoreType.DMA((n,)),
            pltpu.SemaphoreType.DMA((n,)),
            pltpu.SemaphoreType.DMA((n,)),
        ],
        compiler_params=pltpu.CompilerParams(collective_id=0, has_side_effects=True),
    )(blocks, piece)


def gather_kernel(zn, piece_ref, out_ref, send_sem, recv_sem, local_sem):
    row = lax.axis_index("rows")
    col = lax.axis_index("chan")
    b = row % 2
    ylo = (row // 2) % 2
    z = row // 4
    m = ylo * 2 + b
    other = 1 - ylo

    def device(zz, yy, cc):
        return (((zz % zn) * 2 + yy) * 2 + cc, col)

    partner = device(z, ylo, 1 - b)
    ups = device(z + 1, ylo, b)
    downs = device(z + zn - 1, ylo, b)
    side = [device(z, other, c) for c in range(2)]

    barrier = pltpu.get_barrier_semaphore()
    for peer in [partner, ups, downs] + side:
        pl.semaphore_signal(barrier, inc=1, device_id=peer, device_id_type=MESH_ID)
    pl.semaphore_wait(barrier, 5)

    def remote(src, dst, idx, peer, arrival=None):
        arrival = idx if arrival is None else arrival
        return pltpu.make_async_remote_copy(
            src_ref=src, dst_ref=dst, send_sem=send_sem.at[idx], recv_sem=recv_sem.at[arrival],
            device_id=peer, device_id_type=MESH_ID,
        )

    started = []

    def send(src, dst, idx, peer, arrival=None):
        copy = remote(src, dst, idx, peer, arrival)
        copy.start()
        started.append(copy)

    def arrive(dst, idx):
        remote(dst, dst, idx, partner).wait_recv()

    own = []
    for h in range(2):
        copy = pltpu.make_async_copy(piece_ref.at[h], out_ref.at[h, z, m], local_sem.at[h])
        copy.start()
        own.append(copy)
    for h in range(2):
        send(piece_ref.at[h], out_ref.at[h, z, m], h, partner)
    for c in range(2):
        send(piece_ref.at[c], out_ref.at[c, z, m], 2 + c, side[c], 4 + b)
    for copy in own:
        copy.wait()
    arrive(out_ref.at[b, z, ylo * 2 + 1 - b], b)
    arrive(out_ref.at[1 - b, z, ylo * 2 + 1 - b], 1 - b)
    side_slots = pl.ds(other * 2, 2)
    for c in range(2):
        arrive(out_ref.at[b, z, other * 2 + c], 4 + c)
    send(out_ref.at[b, z, side_slots], out_ref.at[b, z, side_slots], 22, partner)

    steps = zn // 2
    rows = piece_ref.shape[1]
    carried = pl.ds(ylo, 3)
    lent = 3 * ylo
    wanted = 3 * other
    up_rows = pl.ds(0, rows // 2)
    down_rows = pl.ds(rows // 2, rows // 2)
    ring_regions = []
    for t in range(1, steps + 1):
        up_block = (z - (t - 1) + zn) % zn
        down_block = (z + (t - 1)) % zn
        if t < steps:
            up_src = out_ref.at[b, up_block, carried]
            down_src = out_ref.at[b, down_block, carried]
        else:
            up_src = out_ref.at[b, up_block, carried, up_rows]
            down_src = out_ref.at[b, down_block, carried, down_rows]
        send(up_src, up_src, 6 + (t - 1), ups)
        send(down_src, down_src, 10 + (t - 1), downs)
        got_up = (z - t + zn) % zn
        got_down = (z + t) % zn
        picks = [(got_up, 6, 14, 23, 31, up_rows), (got_down, 10, 18, 27, 35, down_rows)]
        for block, ring_idx, lend_idx, fwd_idx, fwd_lent_idx, part in picks:
            if t < steps:
                dst = out_ref.at[b, block, carried]
                lend = out_ref.at[b, block, lent]
            else:
                dst = out_ref.at[b, block, carried, part]
                lend = out_ref.at[b, block, lent, part]
            arrive(dst, ring_idx + (t - 1))
            send(lend, lend, lend_idx + (t - 1), device(z, other, b))
            send(dst, dst, fwd_idx + (t - 1), partner)
            ring_regions.append((block, part, ring_idx, lend_idx, fwd_idx, fwd_lent_idx, t))
    for block, part, ring_idx, lend_idx, fwd_idx, fwd_lent_idx, t in ring_regions:
        if t < steps:
            got = out_ref.at[b, block, wanted]
        else:
            got = out_ref.at[b, block, wanted, part]
        arrive(got, lend_idx + (t - 1))
        send(got, got, fwd_lent_idx + (t - 1), partner)

    arrive(out_ref.at[1 - b, z, side_slots], 22)
    for block, part, ring_idx, lend_idx, fwd_idx, fwd_lent_idx, t in ring_regions:
        if t < steps:
            dst = out_ref.at[1 - b, block, carried]
            got = out_ref.at[1 - b, block, wanted]
        else:
            dst = out_ref.at[1 - b, block, carried, part]
            got = out_ref.at[1 - b, block, wanted, part]
        arrive(dst, fwd_idx + (t - 1))
        arrive(got, fwd_lent_idx + (t - 1))
    for copy in started:
        copy.wait_send()


def gather(piece, strips):
    halves, rows, chans = piece.shape
    zn = strips // 4
    sems = 39
    out = pl.pallas_call(
        functools.partial(gather_kernel, zn),
        out_shape=jax.ShapeDtypeStruct((halves, zn, 4, rows, chans), piece.dtype),
        in_specs=[pl.BlockSpec(memory_space=pl.ANY)],
        out_specs=pl.BlockSpec(memory_space=pl.ANY),
        scratch_shapes=[
            pltpu.SemaphoreType.DMA((sems,)),
            pltpu.SemaphoreType.DMA((sems,)),
            pltpu.SemaphoreType.DMA((2,)),
        ],
        compiler_params=pltpu.CompilerParams(collective_id=1, has_side_effects=True),
    )(piece)
    return out.reshape(halves, strips, rows, chans)


def correlate_kernel(factor, x_ref, f_ref, o_ref, acc_ref):
    for s in range(x_ref.shape[0]):
        acc_ref[:, s, :] = jnp.dot(x_ref[s], f_ref[...], preferred_element_type=jnp.float32)
    o_ref[...] = (acc_ref[...] * factor).astype(o_ref.dtype)


def correlate(gathered, queries, factor, share, strips_per_step=16, rows_per_step=320):
    halves, strips, half_rows, chans = gathered.shape
    width = queries.shape[1]
    per_half = half_rows // rows_per_step
    grid = (pl.cdiv(share, rows_per_step), strips // strips_per_step)
    return pl.pallas_call(
        functools.partial(correlate_kernel, factor),
        out_shape=jax.ShapeDtypeStruct((share, strips, width), jnp.bfloat16),
        grid=grid,
        in_specs=[
            pl.BlockSpec(
                (None, strips_per_step, rows_per_step, chans),
                lambda i, j: (i // per_half, j, i % per_half, 0),
            ),
            pl.BlockSpec((chans, width), lambda i, j: (0, 0)),
        ],
        out_specs=pl.BlockSpec((rows_per_step, strips_per_step, width), lambda i, j: (i, j, 0)),
        scratch_shapes=[pltpu.VMEM((rows_per_step, strips_per_step, width), jnp.float32)],
        cost_estimate=pl.CostEstimate(
            flops=2 * strips * share * chans * width,
            bytes_accessed=2 * (strips * share * chans + width * chans + strips * share * width),
            transcendentals=0,
        ),
    )(gathered, queries)


def local(frame_one, frame_two):
    pooled = pool_strip(frame_two)
    groups = lax.axis_size("chan")
    channels = groups * frame_one.shape[1]
    factor = 1.0 / float(channels) ** 0.5
    strips = lax.axis_size("rows")
    share = pooled.shape[0] // groups
    slices = pooled.shape[1]
    blocks = jnp.transpose(pooled.reshape(groups, share, slices), (0, 2, 1))
    traded, pieces = trade(blocks, frame_one.T)
    weights = pieces.reshape(channels, frame_one.shape[0])
    traded = jnp.transpose(traded, (2, 0, 1)).reshape(share, channels)
    padded = -(-share // 320) * 320
    traded = jnp.pad(traded, ((0, padded - share), (0, 0)))
    gathered = gather(traded.reshape(2, padded // 2, channels), strips)
    values = correlate(gathered, weights, factor, share)
    return jnp.transpose(values, (1, 0, 2))


def solution(mesh):
    in_specs = (P("rows", "chan"), P("rows", None, "chan"))
    out_specs = P(None, "chan", "rows")
    return jax.shard_map(local, mesh=mesh, in_specs=in_specs, out_specs=out_specs, check_vma=False)
```

```python
import functools

import jax
import jax.numpy as jnp
from jax import lax
from jax.experimental import pallas as pl
from jax.experimental.pallas import tpu as pltpu
from jax.sharding import PartitionSpec as P

MESH_ID = pl.DeviceIdType.MESH


def pool_strip(strip):
    full = strip.astype(jnp.float32)
    rows_n, cols_n, chans = full.shape
    level_one = full.reshape(rows_n // 2, 2, cols_n // 2, 2, chans).mean(axis=(1, 3))
    level_two = level_one.reshape(rows_n // 4, 2, cols_n // 4, 2, chans).mean(axis=(1, 3))
    joined = jnp.concatenate(
        [full.reshape(-1, chans), level_one.reshape(-1, chans), level_two.reshape(-1, chans)],
        axis=0,
    )
    return joined.astype(jnp.bfloat16)


def trade_kernel(n, x_ref, f_ref, o_ref, g_ref, buf, fbuf, send_sem, recv_sem, fsend_sem, frecv_sem):
    me = lax.axis_index("chan")
    row = lax.axis_index("rows")
    barrier = pltpu.get_barrier_semaphore()
    for k in range(1, n):
        peer = lax.rem(me + k, n)
        pl.semaphore_signal(barrier, inc=1, device_id=(row, peer), device_id_type=MESH_ID)
    pl.semaphore_wait(barrier, n - 1)
    sends = []
    for k in range(1, n):
        peer = lax.rem(me + k, n)
        for src, dst, ssem, rsem in ((x_ref.at[peer], buf.at[me], send_sem, recv_sem), (f_ref, fbuf.at[me], fsend_sem, frecv_sem)):
            copy = pltpu.make_async_remote_copy(
                src_ref=src,
                dst_ref=dst,
                send_sem=ssem.at[k],
                recv_sem=rsem.at[k],
                device_id=(row, peer),
                device_id_type=MESH_ID,
            )
            copy.start()
            sends.append(copy)
    o_ref[me] = x_ref[me]
    g_ref[me] = f_ref[...]
    for k in range(1, n):
        source = lax.rem(me + n - k, n)
        for src, dst, ssem, rsem, out in ((x_ref.at[me], buf.at[source], send_sem, recv_sem, o_ref), (f_ref, fbuf.at[source], fsend_sem, frecv_sem, g_ref)):
            arrival = pltpu.make_async_remote_copy(
                src_ref=src,
                dst_ref=dst,
                send_sem=ssem.at[k],
                recv_sem=rsem.at[k],
                device_id=(row, source),
                device_id_type=MESH_ID,
            )
            arrival.wait_recv()
            out[source] = dst[...]
    for copy in sends:
        copy.wait_send()


def trade(blocks, piece):
    n = blocks.shape[0]
    gathered = (n,) + piece.shape
    return pl.pallas_call(
        functools.partial(trade_kernel, n),
        out_shape=(
            jax.ShapeDtypeStruct(blocks.shape, blocks.dtype),
            jax.ShapeDtypeStruct(gathered, piece.dtype),
        ),
        in_specs=[pl.BlockSpec(memory_space=pltpu.VMEM)] * 2,
        out_specs=(pl.BlockSpec(memory_space=pltpu.VMEM),) * 2,
        scratch_shapes=[
            pltpu.VMEM(blocks.shape, blocks.dtype),
            pltpu.VMEM(gathered, piece.dtype),
            pltpu.SemaphoreType.DMA((n,)),
            pltpu.SemaphoreType.DMA((n,)),
            pltpu.SemaphoreType.DMA((n,)),
            pltpu.SemaphoreType.DMA((n,)),
        ],
        compiler_params=pltpu.CompilerParams(collective_id=0, has_side_effects=True),
    )(blocks, piece)


def gather_kernel(zn, piece_ref, out_ref, send_sem, recv_sem, local_sem):
    row = lax.axis_index("rows")
    col = lax.axis_index("chan")
    b = row % 2
    ylo = (row // 2) % 2
    z = row // 4
    m = ylo * 2 + b
    other = 1 - ylo

    def device(zz, yy, cc):
        return (((zz % zn) * 2 + yy) * 2 + cc, col)

    partner = device(z, ylo, 1 - b)
    ups = device(z + 1, ylo, b)
    downs = device(z + zn - 1, ylo, b)
    side = [device(z, other, c) for c in range(2)]

    barrier = pltpu.get_barrier_semaphore()
    for peer in [partner, ups, downs] + side:
        pl.semaphore_signal(barrier, inc=1, device_id=peer, device_id_type=MESH_ID)
    pl.semaphore_wait(barrier, 5)

    def remote(src, dst, idx, peer, arrival=None):
        arrival = idx if arrival is None else arrival
        return pltpu.make_async_remote_copy(
            src_ref=src, dst_ref=dst, send_sem=send_sem.at[idx], recv_sem=recv_sem.at[arrival],
            device_id=peer, device_id_type=MESH_ID,
        )

    started = []

    def send(src, dst, idx, peer, arrival=None):
        copy = remote(src, dst, idx, peer, arrival)
        copy.start()
        started.append(copy)

    def arrive(dst, idx):
        remote(dst, dst, idx, partner).wait_recv()

    own = []
    for h in range(2):
        copy = pltpu.make_async_copy(piece_ref.at[h], out_ref.at[h, z, m], local_sem.at[h])
        copy.start()
        own.append(copy)
    for h in range(2):
        send(piece_ref.at[h], out_ref.at[h, z, m], h, partner)
    for c in range(2):
        send(piece_ref.at[c], out_ref.at[c, z, m], 2 + c, side[c], 4 + b)
    for copy in own:
        copy.wait()
    arrive(out_ref.at[b, z, ylo * 2 + 1 - b], b)
    arrive(out_ref.at[1 - b, z, ylo * 2 + 1 - b], 1 - b)
    side_slots = pl.ds(other * 2, 2)
    for c in range(2):
        arrive(out_ref.at[b, z, other * 2 + c], 4 + c)
    send(out_ref.at[b, z, side_slots], out_ref.at[b, z, side_slots], 22, partner)

    steps = zn // 2
    rows = piece_ref.shape[1]
    carried = pl.ds(ylo, 3)
    lent = 3 * ylo
    wanted = 3 * other
    up_rows = pl.ds(0, rows // 2)
    down_rows = pl.ds(rows // 2, rows // 2)
    ring_regions = []
    for t in range(1, steps + 1):
        up_block = (z - (t - 1) + zn) % zn
        down_block = (z + (t - 1)) % zn
        if t < steps:
            up_src = out_ref.at[b, up_block, carried]
            down_src = out_ref.at[b, down_block, carried]
        else:
            up_src = out_ref.at[b, up_block, carried, up_rows]
            down_src = out_ref.at[b, down_block, carried, down_rows]
        send(up_src, up_src, 6 + (t - 1), ups)
        send(down_src, down_src, 10 + (t - 1), downs)
        got_up = (z - t + zn) % zn
        got_down = (z + t) % zn
        picks = [(got_up, 6, 14, 23, 31, up_rows), (got_down, 10, 18, 27, 35, down_rows)]
        for block, ring_idx, lend_idx, fwd_idx, fwd_lent_idx, part in picks:
            if t < steps:
                dst = out_ref.at[b, block, carried]
                lend = out_ref.at[b, block, lent]
            else:
                dst = out_ref.at[b, block, carried, part]
                lend = out_ref.at[b, block, lent, part]
            arrive(dst, ring_idx + (t - 1))
            send(lend, lend, lend_idx + (t - 1), device(z, other, b))
            send(dst, dst, fwd_idx + (t - 1), partner)
            ring_regions.append((block, part, ring_idx, lend_idx, fwd_idx, fwd_lent_idx, t))
    for block, part, ring_idx, lend_idx, fwd_idx, fwd_lent_idx, t in ring_regions:
        if t < steps:
            got = out_ref.at[b, block, wanted]
        else:
            got = out_ref.at[b, block, wanted, part]
        arrive(got, lend_idx + (t - 1))
        send(got, got, fwd_lent_idx + (t - 1), partner)

    arrive(out_ref.at[1 - b, z, side_slots], 22)
    for block, part, ring_idx, lend_idx, fwd_idx, fwd_lent_idx, t in ring_regions:
        if t < steps:
            dst = out_ref.at[1 - b, block, carried]
            got = out_ref.at[1 - b, block, wanted]
        else:
            dst = out_ref.at[1 - b, block, carried, part]
            got = out_ref.at[1 - b, block, wanted, part]
        arrive(dst, fwd_idx + (t - 1))
        arrive(got, fwd_lent_idx + (t - 1))
    for copy in started:
        copy.wait_send()


def gather(piece, strips):
    halves, rows, chans = piece.shape
    zn = strips // 4
    sems = 39
    out = pl.pallas_call(
        functools.partial(gather_kernel, zn),
        out_shape=jax.ShapeDtypeStruct((halves, zn, 4, rows, chans), piece.dtype),
        in_specs=[pl.BlockSpec(memory_space=pltpu.VMEM)],
        out_specs=pl.BlockSpec(memory_space=pl.ANY),
        scratch_shapes=[
            pltpu.SemaphoreType.DMA((sems,)),
            pltpu.SemaphoreType.DMA((sems,)),
            pltpu.SemaphoreType.DMA((2,)),
        ],
        compiler_params=pltpu.CompilerParams(collective_id=1, has_side_effects=True),
    )(piece)
    return out.reshape(halves, strips, rows, chans)


def correlate_kernel(factor, x_ref, f_ref, o_ref, acc_ref):
    for s in range(x_ref.shape[0]):
        acc_ref[:, s, :] = jnp.dot(x_ref[s], f_ref[...], preferred_element_type=jnp.float32)
    o_ref[...] = (acc_ref[...] * factor).astype(o_ref.dtype)


def correlate(gathered, queries, factor, share, strips_per_step=16, rows_per_step=320):
    halves, strips, half_rows, chans = gathered.shape
    width = queries.shape[1]
    per_half = half_rows // rows_per_step
    grid = (pl.cdiv(share, rows_per_step), strips // strips_per_step)
    return pl.pallas_call(
        functools.partial(correlate_kernel, factor),
        out_shape=jax.ShapeDtypeStruct((share, strips, width), jnp.bfloat16),
        grid=grid,
        in_specs=[
            pl.BlockSpec(
                (None, strips_per_step, rows_per_step, chans),
                lambda i, j: (i // per_half, j, i % per_half, 0),
            ),
            pl.BlockSpec((chans, width), lambda i, j: (0, 0)),
        ],
        out_specs=pl.BlockSpec((rows_per_step, strips_per_step, width), lambda i, j: (i, j, 0)),
        scratch_shapes=[pltpu.VMEM((rows_per_step, strips_per_step, width), jnp.float32)],
        cost_estimate=pl.CostEstimate(
            flops=2 * strips * share * chans * width,
            bytes_accessed=2 * (strips * share * chans + width * chans + strips * share * width),
            transcendentals=0,
        ),
    )(gathered, queries)


def local(frame_one, frame_two):
    pooled = pool_strip(frame_two)
    groups = lax.axis_size("chan")
    channels = groups * frame_one.shape[1]
    factor = 1.0 / float(channels) ** 0.5
    strips = lax.axis_size("rows")
    share = pooled.shape[0] // groups
    slices = pooled.shape[1]
    blocks = jnp.transpose(pooled.reshape(groups, share, slices), (0, 2, 1))
    traded, pieces = trade(blocks, frame_one.T)
    weights = pieces.reshape(channels, frame_one.shape[0])
    traded = jnp.transpose(traded, (2, 0, 1)).reshape(share, channels)
    padded = -(-share // 320) * 320
    traded = jnp.pad(traded, ((0, padded - share), (0, 0)))
    gathered = gather(traded.reshape(2, padded // 2, channels), strips)
    values = correlate(gathered, weights, factor, share)
    return jnp.transpose(values, (1, 0, 2))


def solution(mesh):
    in_specs = (P("rows", "chan"), P("rows", None, "chan"))
    out_specs = P(None, "chan", "rows")
    return jax.shard_map(local, mesh=mesh, in_specs=in_specs, out_specs=out_specs, check_vma=False)
```

```python
import functools

import jax
import jax.numpy as jnp
from jax import lax
from jax.experimental import pallas as pl
from jax.experimental.pallas import tpu as pltpu
from jax.sharding import PartitionSpec as P

MESH_ID = pl.DeviceIdType.MESH


def pool_strip(strip):
    full = strip.astype(jnp.float32)
    rows_n, cols_n, chans = full.shape
    level_one = full.reshape(rows_n // 2, 2, cols_n // 2, 2, chans).mean(axis=(1, 3))
    level_two = level_one.reshape(rows_n // 4, 2, cols_n // 4, 2, chans).mean(axis=(1, 3))
    joined = jnp.concatenate(
        [full.reshape(-1, chans), level_one.reshape(-1, chans), level_two.reshape(-1, chans)],
        axis=0,
    )
    return joined.astype(jnp.bfloat16)


def trade_kernel(n, x_ref, f_ref, o_ref, g_ref, buf, fbuf, send_sem, recv_sem, fsend_sem, frecv_sem):
    me = lax.axis_index("chan")
    row = lax.axis_index("rows")
    barrier = pltpu.get_barrier_semaphore()
    for k in range(1, n):
        peer = lax.rem(me + k, n)
        pl.semaphore_signal(barrier, inc=1, device_id=(row, peer), device_id_type=MESH_ID)
    pl.semaphore_wait(barrier, n - 1)
    sends = []
    for k in range(1, n):
        peer = lax.rem(me + k, n)
        for src, dst, ssem, rsem in ((x_ref.at[peer], buf.at[me], send_sem, recv_sem), (f_ref, fbuf.at[me], fsend_sem, frecv_sem)):
            copy = pltpu.make_async_remote_copy(
                src_ref=src,
                dst_ref=dst,
                send_sem=ssem.at[k],
                recv_sem=rsem.at[k],
                device_id=(row, peer),
                device_id_type=MESH_ID,
            )
            copy.start()
            sends.append(copy)
    o_ref[me] = x_ref[me]
    g_ref[me] = f_ref[...]
    for k in range(1, n):
        source = lax.rem(me + n - k, n)
        for src, dst, ssem, rsem, out in ((x_ref.at[me], buf.at[source], send_sem, recv_sem, o_ref), (f_ref, fbuf.at[source], fsend_sem, frecv_sem, g_ref)):
            arrival = pltpu.make_async_remote_copy(
                src_ref=src,
                dst_ref=dst,
                send_sem=ssem.at[k],
                recv_sem=rsem.at[k],
                device_id=(row, source),
                device_id_type=MESH_ID,
            )
            arrival.wait_recv()
            out[source] = dst[...]
    for copy in sends:
        copy.wait_send()


def trade(blocks, piece):
    n = blocks.shape[0]
    gathered = (n,) + piece.shape
    return pl.pallas_call(
        functools.partial(trade_kernel, n),
        out_shape=(
            jax.ShapeDtypeStruct(blocks.shape, blocks.dtype),
            jax.ShapeDtypeStruct(gathered, piece.dtype),
        ),
        in_specs=[pl.BlockSpec(memory_space=pltpu.VMEM)] * 2,
        out_specs=(pl.BlockSpec(memory_space=pltpu.VMEM),) * 2,
        scratch_shapes=[
            pltpu.VMEM(blocks.shape, blocks.dtype),
            pltpu.VMEM(gathered, piece.dtype),
            pltpu.SemaphoreType.DMA((n,)),
            pltpu.SemaphoreType.DMA((n,)),
            pltpu.SemaphoreType.DMA((n,)),
            pltpu.SemaphoreType.DMA((n,)),
        ],
        compiler_params=pltpu.CompilerParams(collective_id=0, has_side_effects=True),
    )(blocks, piece)


def gather_kernel(zn, piece_ref, out_ref, send_sem, recv_sem, local_sem):
    row = lax.axis_index("rows")
    col = lax.axis_index("chan")
    b = row % 2
    ylo = (row // 2) % 2
    z = row // 4
    m = ylo * 2 + b
    other = 1 - ylo

    def device(zz, yy, cc):
        return (((zz % zn) * 2 + yy) * 2 + cc, col)

    partner = device(z, ylo, 1 - b)
    ups = device(z + 1, ylo, b)
    downs = device(z + zn - 1, ylo, b)
    side = [device(z, other, c) for c in range(2)]

    barrier = pltpu.get_barrier_semaphore()
    for peer in [partner, ups, downs] + side:
        pl.semaphore_signal(barrier, inc=1, device_id=peer, device_id_type=MESH_ID)
    pl.semaphore_wait(barrier, 5)

    def remote(src, dst, idx, peer, arrival=None):
        arrival = idx if arrival is None else arrival
        return pltpu.make_async_remote_copy(
            src_ref=src, dst_ref=dst, send_sem=send_sem.at[idx], recv_sem=recv_sem.at[arrival],
            device_id=peer, device_id_type=MESH_ID,
        )

    started = []

    def send(src, dst, idx, peer, arrival=None):
        copy = remote(src, dst, idx, peer, arrival)
        copy.start()
        started.append(copy)

    def arrive(dst, idx):
        remote(dst, dst, idx, partner).wait_recv()

    own = []
    for h in range(2):
        copy = pltpu.make_async_copy(piece_ref.at[h], out_ref.at[h, z, m], local_sem.at[h])
        copy.start()
        own.append(copy)
    for h in range(2):
        send(piece_ref.at[h], out_ref.at[h, z, m], h, partner)
    for c in range(2):
        send(piece_ref.at[c], out_ref.at[c, z, m], 2 + c, side[c], 4 + b)
    for copy in own:
        copy.wait()
    arrive(out_ref.at[b, z, ylo * 2 + 1 - b], b)
    arrive(out_ref.at[1 - b, z, ylo * 2 + 1 - b], 1 - b)
    side_slots = pl.ds(other * 2, 2)
    for c in range(2):
        arrive(out_ref.at[b, z, other * 2 + c], 4 + c)
    send(out_ref.at[b, z, side_slots], out_ref.at[b, z, side_slots], 22, partner)

    steps = zn // 2
    rows = piece_ref.shape[1]
    carried = pl.ds(ylo, 3)
    lent = 3 * ylo
    wanted = 3 * other
    up_rows = pl.ds(0, rows // 2)
    down_rows = pl.ds(rows // 2, rows // 2)
    ring_regions = []

    def send_ring(up, t):
        if up:
            block = (z - (t - 1) + zn) % zn
            part, idx, peer = up_rows, 6, ups
        else:
            block = (z + (t - 1)) % zn
            part, idx, peer = down_rows, 10, downs
        if t < steps:
            src = out_ref.at[b, block, carried]
        else:
            src = out_ref.at[b, block, carried, part]
        send(src, src, idx + (t - 1), peer)

    send_ring(True, 1)
    send_ring(False, 1)
    for t in range(1, steps + 1):
        got_up = (z - t + zn) % zn
        got_down = (z + t) % zn
        picks = [(True, got_up, 6, 14, 23, 31, up_rows), (False, got_down, 10, 18, 27, 35, down_rows)]
        for up, block, ring_idx, lend_idx, fwd_idx, fwd_lent_idx, part in picks:
            if t < steps:
                dst = out_ref.at[b, block, carried]
                lend = out_ref.at[b, block, lent]
            else:
                dst = out_ref.at[b, block, carried, part]
                lend = out_ref.at[b, block, lent, part]
            arrive(dst, ring_idx + (t - 1))
            if t < steps:
                send_ring(up, t + 1)
            send(lend, lend, lend_idx + (t - 1), device(z, other, b))
            send(dst, dst, fwd_idx + (t - 1), partner)
            ring_regions.append((block, part, ring_idx, lend_idx, fwd_idx, fwd_lent_idx, t))
    for block, part, ring_idx, lend_idx, fwd_idx, fwd_lent_idx, t in ring_regions:
        if t < steps:
            got = out_ref.at[b, block, wanted]
        else:
            got = out_ref.at[b, block, wanted, part]
        arrive(got, lend_idx + (t - 1))
        send(got, got, fwd_lent_idx + (t - 1), partner)

    arrive(out_ref.at[1 - b, z, side_slots], 22)
    for block, part, ring_idx, lend_idx, fwd_idx, fwd_lent_idx, t in ring_regions:
        if t < steps:
            dst = out_ref.at[1 - b, block, carried]
            got = out_ref.at[1 - b, block, wanted]
        else:
            dst = out_ref.at[1 - b, block, carried, part]
            got = out_ref.at[1 - b, block, wanted, part]
        arrive(dst, fwd_idx + (t - 1))
        arrive(got, fwd_lent_idx + (t - 1))
    for copy in started:
        copy.wait_send()


def gather(piece, strips):
    halves, rows, chans = piece.shape
    zn = strips // 4
    sems = 39
    out = pl.pallas_call(
        functools.partial(gather_kernel, zn),
        out_shape=jax.ShapeDtypeStruct((halves, zn, 4, rows, chans), piece.dtype),
        in_specs=[pl.BlockSpec(memory_space=pltpu.VMEM)],
        out_specs=pl.BlockSpec(memory_space=pl.ANY),
        scratch_shapes=[
            pltpu.SemaphoreType.DMA((sems,)),
            pltpu.SemaphoreType.DMA((sems,)),
            pltpu.SemaphoreType.DMA((2,)),
        ],
        compiler_params=pltpu.CompilerParams(collective_id=1, has_side_effects=True),
    )(piece)
    return out.reshape(halves, strips, rows, chans)


def correlate_kernel(factor, x_ref, f_ref, o_ref, acc_ref):
    for s in range(x_ref.shape[0]):
        acc_ref[:, s, :] = jnp.dot(x_ref[s], f_ref[...], preferred_element_type=jnp.float32)
    o_ref[...] = (acc_ref[...] * factor).astype(o_ref.dtype)


def correlate(gathered, queries, factor, share, strips_per_step=16, rows_per_step=320):
    halves, strips, half_rows, chans = gathered.shape
    width = queries.shape[1]
    per_half = half_rows // rows_per_step
    grid = (pl.cdiv(share, rows_per_step), strips // strips_per_step)
    return pl.pallas_call(
        functools.partial(correlate_kernel, factor),
        out_shape=jax.ShapeDtypeStruct((share, strips, width), jnp.bfloat16),
        grid=grid,
        in_specs=[
            pl.BlockSpec(
                (None, strips_per_step, rows_per_step, chans),
                lambda i, j: (i // per_half, j, i % per_half, 0),
            ),
            pl.BlockSpec((chans, width), lambda i, j: (0, 0)),
        ],
        out_specs=pl.BlockSpec((rows_per_step, strips_per_step, width), lambda i, j: (i, j, 0)),
        scratch_shapes=[pltpu.VMEM((rows_per_step, strips_per_step, width), jnp.float32)],
        cost_estimate=pl.CostEstimate(
            flops=2 * strips * share * chans * width,
            bytes_accessed=2 * (strips * share * chans + width * chans + strips * share * width),
            transcendentals=0,
        ),
    )(gathered, queries)


def local(frame_one, frame_two):
    pooled = pool_strip(frame_two)
    groups = lax.axis_size("chan")
    channels = groups * frame_one.shape[1]
    factor = 1.0 / float(channels) ** 0.5
    strips = lax.axis_size("rows")
    share = pooled.shape[0] // groups
    slices = pooled.shape[1]
    blocks = jnp.transpose(pooled.reshape(groups, share, slices), (0, 2, 1))
    traded, pieces = trade(blocks, frame_one.T)
    weights = pieces.reshape(channels, frame_one.shape[0])
    traded = jnp.transpose(traded, (2, 0, 1)).reshape(share, channels)
    padded = -(-share // 320) * 320
    traded = jnp.pad(traded, ((0, padded - share), (0, 0)))
    gathered = gather(traded.reshape(2, padded // 2, channels), strips)
    values = correlate(gathered, weights, factor, share)
    return jnp.transpose(values, (1, 0, 2))


def solution(mesh):
    in_specs = (P("rows", "chan"), P("rows", None, "chan"))
    out_specs = P(None, "chan", "rows")
    return jax.shard_map(local, mesh=mesh, in_specs=in_specs, out_specs=out_specs, check_vma=False)
```

```python
import functools

import jax
import jax.numpy as jnp
from jax import lax
from jax.experimental import pallas as pl
from jax.experimental.pallas import tpu as pltpu
from jax.sharding import PartitionSpec as P

MESH_ID = pl.DeviceIdType.MESH


def pool_strip(strip):
    full = strip.astype(jnp.float32)
    rows_n, cols_n, chans = full.shape
    level_one = full.reshape(rows_n // 2, 2, cols_n // 2, 2, chans).mean(axis=(1, 3))
    level_two = level_one.reshape(rows_n // 4, 2, cols_n // 4, 2, chans).mean(axis=(1, 3))
    joined = jnp.concatenate(
        [full.reshape(-1, chans), level_one.reshape(-1, chans), level_two.reshape(-1, chans)],
        axis=0,
    )
    return joined.astype(jnp.bfloat16)


def trade_kernel(n, x_ref, f_ref, o_ref, g_ref, buf, fbuf, send_sem, recv_sem, fsend_sem, frecv_sem):
    me = lax.axis_index("chan")
    row = lax.axis_index("rows")
    barrier = pltpu.get_barrier_semaphore()
    for k in range(1, n):
        peer = lax.rem(me + k, n)
        pl.semaphore_signal(barrier, inc=1, device_id=(row, peer), device_id_type=MESH_ID)
    pl.semaphore_wait(barrier, n - 1)
    sends = []
    for k in range(1, n):
        peer = lax.rem(me + k, n)
        for src, dst, ssem, rsem in ((x_ref.at[peer], buf.at[me], send_sem, recv_sem), (f_ref, fbuf.at[me], fsend_sem, frecv_sem)):
            copy = pltpu.make_async_remote_copy(
                src_ref=src,
                dst_ref=dst,
                send_sem=ssem.at[k],
                recv_sem=rsem.at[k],
                device_id=(row, peer),
                device_id_type=MESH_ID,
            )
            copy.start()
            sends.append(copy)
    o_ref[me] = x_ref[me]
    g_ref[me] = f_ref[...]
    for k in range(1, n):
        source = lax.rem(me + n - k, n)
        for src, dst, ssem, rsem, out in ((x_ref.at[me], buf.at[source], send_sem, recv_sem, o_ref), (f_ref, fbuf.at[source], fsend_sem, frecv_sem, g_ref)):
            arrival = pltpu.make_async_remote_copy(
                src_ref=src,
                dst_ref=dst,
                send_sem=ssem.at[k],
                recv_sem=rsem.at[k],
                device_id=(row, source),
                device_id_type=MESH_ID,
            )
            arrival.wait_recv()
            out[source] = dst[...]
    for copy in sends:
        copy.wait_send()


def trade(blocks, piece):
    n = blocks.shape[0]
    gathered = (n,) + piece.shape
    return pl.pallas_call(
        functools.partial(trade_kernel, n),
        out_shape=(
            jax.ShapeDtypeStruct(blocks.shape, blocks.dtype),
            jax.ShapeDtypeStruct(gathered, piece.dtype),
        ),
        in_specs=[pl.BlockSpec(memory_space=pltpu.VMEM)] * 2,
        out_specs=(pl.BlockSpec(memory_space=pltpu.VMEM),) * 2,
        scratch_shapes=[
            pltpu.VMEM(blocks.shape, blocks.dtype),
            pltpu.VMEM(gathered, piece.dtype),
            pltpu.SemaphoreType.DMA((n,)),
            pltpu.SemaphoreType.DMA((n,)),
            pltpu.SemaphoreType.DMA((n,)),
            pltpu.SemaphoreType.DMA((n,)),
        ],
        compiler_params=pltpu.CompilerParams(collective_id=0, has_side_effects=True),
    )(blocks, piece)


def gather_kernel(zn, piece_ref, out_ref, send_sem, recv_sem, local_sem):
    row = lax.axis_index("rows")
    col = lax.axis_index("chan")
    b = row % 2
    ylo = (row // 2) % 2
    z = row // 4
    m = ylo * 2 + b
    other = 1 - ylo

    def device(zz, yy, cc):
        return (((zz % zn) * 2 + yy) * 2 + cc, col)

    partner = device(z, ylo, 1 - b)
    ups = device(z + 1, ylo, b)
    downs = device(z + zn - 1, ylo, b)
    side = [device(z, other, c) for c in range(2)]

    barrier = pltpu.get_barrier_semaphore()
    for peer in [partner, ups, downs] + side:
        pl.semaphore_signal(barrier, inc=1, device_id=peer, device_id_type=MESH_ID)
    pl.semaphore_wait(barrier, 5)

    def remote(src, dst, idx, peer, arrival=None):
        arrival = idx if arrival is None else arrival
        return pltpu.make_async_remote_copy(
            src_ref=src, dst_ref=dst, send_sem=send_sem.at[idx], recv_sem=recv_sem.at[arrival],
            device_id=peer, device_id_type=MESH_ID,
        )

    started = []

    def send(src, dst, idx, peer, arrival=None):
        copy = remote(src, dst, idx, peer, arrival)
        copy.start()
        started.append(copy)

    def arrive(dst, idx):
        remote(dst, dst, idx, partner).wait_recv()

    own = []
    for h in range(2):
        copy = pltpu.make_async_copy(piece_ref.at[h], out_ref.at[h, z, m], local_sem.at[h])
        copy.start()
        own.append(copy)
    for h in range(2):
        send(piece_ref.at[h], out_ref.at[h, z, m], h, partner)
    for c in range(2):
        send(piece_ref.at[c], out_ref.at[c, z, m], 2 + c, side[c], 4 + b)
    for copy in own:
        copy.wait()
    arrive(out_ref.at[b, z, ylo * 2 + 1 - b], b)
    arrive(out_ref.at[b, z, other * 2 + ylo], 4 + ylo)
    side_slots = pl.ds(other * 2, 2)

    steps = zn // 2
    rows = piece_ref.shape[1]
    carried = pl.ds(ylo, 3)
    lent = 3 * ylo
    wanted = 3 * other
    up_rows = pl.ds(0, rows // 2)
    down_rows = pl.ds(rows // 2, rows // 2)
    ring_regions = []

    def send_ring(up, t):
        if up:
            block = (z - (t - 1) + zn) % zn
            part, idx, peer = up_rows, 6, ups
        else:
            block = (z + (t - 1)) % zn
            part, idx, peer = down_rows, 10, downs
        if t < steps:
            src = out_ref.at[b, block, carried]
        else:
            src = out_ref.at[b, block, carried, part]
        send(src, src, idx + (t - 1), peer)

    send_ring(True, 1)
    send_ring(False, 1)
    arrive(out_ref.at[1 - b, z, ylo * 2 + 1 - b], 1 - b)
    arrive(out_ref.at[b, z, other * 2 + 1 - ylo], 5 - ylo)
    send(out_ref.at[b, z, side_slots], out_ref.at[b, z, side_slots], 22, partner)
    for t in range(1, steps + 1):
        got_up = (z - t + zn) % zn
        got_down = (z + t) % zn
        picks = [(True, got_up, 6, 14, 23, 31, up_rows), (False, got_down, 10, 18, 27, 35, down_rows)]
        for up, block, ring_idx, lend_idx, fwd_idx, fwd_lent_idx, part in picks:
            if t < steps:
                dst = out_ref.at[b, block, carried]
                lend = out_ref.at[b, block, lent]
            else:
                dst = out_ref.at[b, block, carried, part]
                lend = out_ref.at[b, block, lent, part]
            arrive(dst, ring_idx + (t - 1))
            if t < steps:
                send_ring(up, t + 1)
            send(lend, lend, lend_idx + (t - 1), device(z, other, b))
            send(dst, dst, fwd_idx + (t - 1), partner)
            ring_regions.append((block, part, ring_idx, lend_idx, fwd_idx, fwd_lent_idx, t))
    for block, part, ring_idx, lend_idx, fwd_idx, fwd_lent_idx, t in ring_regions:
        if t < steps:
            got = out_ref.at[b, block, wanted]
        else:
            got = out_ref.at[b, block, wanted, part]
        arrive(got, lend_idx + (t - 1))
        send(got, got, fwd_lent_idx + (t - 1), partner)

    arrive(out_ref.at[1 - b, z, side_slots], 22)
    for block, part, ring_idx, lend_idx, fwd_idx, fwd_lent_idx, t in ring_regions:
        if t < steps:
            dst = out_ref.at[1 - b, block, carried]
            got = out_ref.at[1 - b, block, wanted]
        else:
            dst = out_ref.at[1 - b, block, carried, part]
            got = out_ref.at[1 - b, block, wanted, part]
        arrive(dst, fwd_idx + (t - 1))
        arrive(got, fwd_lent_idx + (t - 1))
    for copy in started:
        copy.wait_send()


def gather(piece, strips):
    halves, rows, chans = piece.shape
    zn = strips // 4
    sems = 39
    out = pl.pallas_call(
        functools.partial(gather_kernel, zn),
        out_shape=jax.ShapeDtypeStruct((halves, zn, 4, rows, chans), piece.dtype),
        in_specs=[pl.BlockSpec(memory_space=pltpu.VMEM)],
        out_specs=pl.BlockSpec(memory_space=pl.ANY),
        scratch_shapes=[
            pltpu.SemaphoreType.DMA((sems,)),
            pltpu.SemaphoreType.DMA((sems,)),
            pltpu.SemaphoreType.DMA((2,)),
        ],
        compiler_params=pltpu.CompilerParams(collective_id=1, has_side_effects=True),
    )(piece)
    return out.reshape(halves, strips, rows, chans)


def correlate_kernel(factor, x_ref, f_ref, o_ref, acc_ref):
    for s in range(x_ref.shape[0]):
        acc_ref[:, s, :] = jnp.dot(x_ref[s], f_ref[...], preferred_element_type=jnp.float32)
    o_ref[...] = (acc_ref[...] * factor).astype(o_ref.dtype)


def correlate(gathered, queries, factor, share, strips_per_step=16, rows_per_step=320):
    halves, strips, half_rows, chans = gathered.shape
    width = queries.shape[1]
    per_half = half_rows // rows_per_step
    grid = (pl.cdiv(share, rows_per_step), strips // strips_per_step)
    return pl.pallas_call(
        functools.partial(correlate_kernel, factor),
        out_shape=jax.ShapeDtypeStruct((share, strips, width), jnp.bfloat16),
        grid=grid,
        in_specs=[
            pl.BlockSpec(
                (None, strips_per_step, rows_per_step, chans),
                lambda i, j: (i // per_half, j, i % per_half, 0),
            ),
            pl.BlockSpec((chans, width), lambda i, j: (0, 0)),
        ],
        out_specs=pl.BlockSpec((rows_per_step, strips_per_step, width), lambda i, j: (i, j, 0)),
        scratch_shapes=[pltpu.VMEM((rows_per_step, strips_per_step, width), jnp.float32)],
        cost_estimate=pl.CostEstimate(
            flops=2 * strips * share * chans * width,
            bytes_accessed=2 * (strips * share * chans + width * chans + strips * share * width),
            transcendentals=0,
        ),
    )(gathered, queries)


def local(frame_one, frame_two):
    pooled = pool_strip(frame_two)
    groups = lax.axis_size("chan")
    channels = groups * frame_one.shape[1]
    factor = 1.0 / float(channels) ** 0.5
    strips = lax.axis_size("rows")
    share = pooled.shape[0] // groups
    slices = pooled.shape[1]
    blocks = jnp.transpose(pooled.reshape(groups, share, slices), (0, 2, 1))
    traded, pieces = trade(blocks, frame_one.T)
    weights = pieces.reshape(channels, frame_one.shape[0])
    traded = jnp.transpose(traded, (2, 0, 1)).reshape(share, channels)
    padded = -(-share // 320) * 320
    traded = jnp.pad(traded, ((0, padded - share), (0, 0)))
    gathered = gather(traded.reshape(2, padded // 2, channels), strips)
    values = correlate(gathered, weights, factor, share)
    return jnp.transpose(values, (1, 0, 2))


def solution(mesh):
    in_specs = (P("rows", "chan"), P("rows", None, "chan"))
    out_specs = P(None, "chan", "rows")
    return jax.shard_map(local, mesh=mesh, in_specs=in_specs, out_specs=out_specs, check_vma=False)
```

```python
import functools

import jax
import jax.numpy as jnp
from jax import lax
from jax.experimental import pallas as pl
from jax.experimental.pallas import tpu as pltpu
from jax.sharding import PartitionSpec as P

MESH_ID = pl.DeviceIdType.MESH


def pool_strip(strip):
    full = strip.astype(jnp.float32)
    rows_n, cols_n, chans = full.shape
    level_one = full.reshape(rows_n // 2, 2, cols_n // 2, 2, chans).mean(axis=(1, 3))
    level_two = level_one.reshape(rows_n // 4, 2, cols_n // 4, 2, chans).mean(axis=(1, 3))
    joined = jnp.concatenate(
        [full.reshape(-1, chans), level_one.reshape(-1, chans), level_two.reshape(-1, chans)],
        axis=0,
    )
    return joined.astype(jnp.bfloat16)


def trade_kernel(n, x_ref, f_ref, o_ref, g_ref, buf, fbuf, send_sem, recv_sem, fsend_sem, frecv_sem):
    me = lax.axis_index("chan")
    row = lax.axis_index("rows")
    barrier = pltpu.get_barrier_semaphore()
    for k in range(1, n):
        peer = lax.rem(me + k, n)
        pl.semaphore_signal(barrier, inc=1, device_id=(row, peer), device_id_type=MESH_ID)
    pl.semaphore_wait(barrier, n - 1)
    sends = []
    for k in range(1, n):
        peer = lax.rem(me + k, n)
        for src, dst, ssem, rsem in ((x_ref.at[peer], buf.at[me], send_sem, recv_sem), (f_ref, fbuf.at[me], fsend_sem, frecv_sem)):
            copy = pltpu.make_async_remote_copy(
                src_ref=src,
                dst_ref=dst,
                send_sem=ssem.at[k],
                recv_sem=rsem.at[k],
                device_id=(row, peer),
                device_id_type=MESH_ID,
            )
            copy.start()
            sends.append(copy)
    o_ref[me] = x_ref[me]
    g_ref[me] = f_ref[...]
    for k in range(1, n):
        source = lax.rem(me + n - k, n)
        for src, dst, ssem, rsem, out in ((x_ref.at[me], buf.at[source], send_sem, recv_sem, o_ref), (f_ref, fbuf.at[source], fsend_sem, frecv_sem, g_ref)):
            arrival = pltpu.make_async_remote_copy(
                src_ref=src,
                dst_ref=dst,
                send_sem=ssem.at[k],
                recv_sem=rsem.at[k],
                device_id=(row, source),
                device_id_type=MESH_ID,
            )
            arrival.wait_recv()
            out[source] = dst[...]
    for copy in sends:
        copy.wait_send()


def trade(blocks, piece):
    n = blocks.shape[0]
    gathered = (n,) + piece.shape
    return pl.pallas_call(
        functools.partial(trade_kernel, n),
        out_shape=(
            jax.ShapeDtypeStruct(blocks.shape, blocks.dtype),
            jax.ShapeDtypeStruct(gathered, piece.dtype),
        ),
        in_specs=[pl.BlockSpec(memory_space=pltpu.VMEM)] * 2,
        out_specs=(pl.BlockSpec(memory_space=pltpu.VMEM),) * 2,
        scratch_shapes=[
            pltpu.VMEM(blocks.shape, blocks.dtype),
            pltpu.VMEM(gathered, piece.dtype),
            pltpu.SemaphoreType.DMA((n,)),
            pltpu.SemaphoreType.DMA((n,)),
            pltpu.SemaphoreType.DMA((n,)),
            pltpu.SemaphoreType.DMA((n,)),
        ],
        compiler_params=pltpu.CompilerParams(collective_id=0, has_side_effects=True),
    )(blocks, piece)


def gather_kernel(zn, piece_ref, out_ref, send_sem, recv_sem, local_sem):
    row = lax.axis_index("rows")
    col = lax.axis_index("chan")
    b = row % 2
    ylo = (row // 2) % 2
    z = row // 4
    m = ylo * 2 + b
    other = 1 - ylo

    def device(zz, yy, cc):
        return (((zz % zn) * 2 + yy) * 2 + cc, col)

    partner = device(z, ylo, 1 - b)
    ups = device(z + 1, ylo, b)
    downs = device(z + zn - 1, ylo, b)
    side = [device(z, other, c) for c in range(2)]

    barrier = pltpu.get_barrier_semaphore()
    for peer in [partner, ups, downs] + side:
        pl.semaphore_signal(barrier, inc=1, device_id=peer, device_id_type=MESH_ID)
    pl.semaphore_wait(barrier, 5)

    def remote(src, dst, idx, peer, arrival=None):
        arrival = idx if arrival is None else arrival
        return pltpu.make_async_remote_copy(
            src_ref=src, dst_ref=dst, send_sem=send_sem.at[idx], recv_sem=recv_sem.at[arrival],
            device_id=peer, device_id_type=MESH_ID,
        )

    started = []

    def send(src, dst, idx, peer, arrival=None):
        copy = remote(src, dst, idx, peer, arrival)
        copy.start()
        started.append(copy)

    def arrive(dst, idx):
        remote(dst, dst, idx, partner).wait_recv()

    own = []
    for h in range(2):
        copy = pltpu.make_async_copy(piece_ref.at[h], out_ref.at[h, z, m], local_sem.at[h])
        copy.start()
        own.append(copy)
    for h in range(2):
        send(piece_ref.at[h], out_ref.at[h, z, m], h, partner)
    for c in range(2):
        send(piece_ref.at[c], out_ref.at[c, z, m], 2 + c, side[c], 4 + b)
    for copy in own:
        copy.wait()
    arrive(out_ref.at[b, z, ylo * 2 + 1 - b], b)
    arrive(out_ref.at[b, z, other * 2 + ylo], 4 + ylo)
    side_slots = pl.ds(other * 2, 2)

    steps = zn // 2
    rows = piece_ref.shape[1]
    carried = pl.ds(ylo, 3)
    lent = 3 * ylo
    wanted = 3 * other
    up_rows = pl.ds(0, rows // 2)
    down_rows = pl.ds(rows // 2, rows // 2)
    ring_regions = []

    def send_ring(up, t):
        if up:
            block = (z - (t - 1) + zn) % zn
            part, idx, peer = up_rows, 6, ups
        else:
            block = (z + (t - 1)) % zn
            part, idx, peer = down_rows, 10, downs
        if t < steps:
            src = out_ref.at[b, block, carried]
        else:
            src = out_ref.at[b, block, carried, part]
        send(src, src, idx + (t - 1), peer)

    send_ring(True, 1)
    send_ring(False, 1)
    arrive(out_ref.at[1 - b, z, ylo * 2 + 1 - b], 1 - b)
    arrive(out_ref.at[b, z, other * 2 + 1 - ylo], 5 - ylo)
    send(out_ref.at[b, z, side_slots], out_ref.at[b, z, side_slots], 22, partner)
    for t in range(1, steps + 1):
        got_up = (z - t + zn) % zn
        got_down = (z + t) % zn
        picks = [(True, got_up, 6, 14, 23, 31, up_rows), (False, got_down, 10, 18, 27, 35, down_rows)]
        for up, block, ring_idx, lend_idx, fwd_idx, fwd_lent_idx, part in picks:
            if t < steps:
                dst = out_ref.at[b, block, carried]
                lend = out_ref.at[b, block, lent]
            else:
                dst = out_ref.at[b, block, carried, part]
                lend = out_ref.at[b, block, lent, part]
            arrive(dst, ring_idx + (t - 1))
            if t < steps:
                send_ring(up, t + 1)
            send(lend, lend, lend_idx + (t - 1), device(z, other, b))
            send(dst, dst, fwd_idx + (t - 1), partner)
            ring_regions.append((block, part, ring_idx, lend_idx, fwd_idx, fwd_lent_idx, t))
    for block, part, ring_idx, lend_idx, fwd_idx, fwd_lent_idx, t in ring_regions:
        if t < steps:
            got = out_ref.at[b, block, wanted]
        else:
            got = out_ref.at[b, block, wanted, part]
        arrive(got, lend_idx + (t - 1))
        send(got, got, fwd_lent_idx + (t - 1), partner)

    arrive(out_ref.at[1 - b, z, side_slots], 22)
    for block, part, ring_idx, lend_idx, fwd_idx, fwd_lent_idx, t in ring_regions:
        if t < steps:
            dst = out_ref.at[1 - b, block, carried]
            got = out_ref.at[1 - b, block, wanted]
        else:
            dst = out_ref.at[1 - b, block, carried, part]
            got = out_ref.at[1 - b, block, wanted, part]
        arrive(dst, fwd_idx + (t - 1))
        arrive(got, fwd_lent_idx + (t - 1))
    for copy in started:
        copy.wait_send()


def gather(piece, strips):
    halves, rows, chans = piece.shape
    zn = strips // 4
    sems = 39
    out = pl.pallas_call(
        functools.partial(gather_kernel, zn),
        out_shape=jax.ShapeDtypeStruct((halves, zn, 4, rows, chans), piece.dtype),
        in_specs=[pl.BlockSpec(memory_space=pltpu.VMEM)],
        out_specs=pl.BlockSpec(memory_space=pl.ANY),
        scratch_shapes=[
            pltpu.SemaphoreType.DMA((sems,)),
            pltpu.SemaphoreType.DMA((sems,)),
            pltpu.SemaphoreType.DMA((2,)),
        ],
        compiler_params=pltpu.CompilerParams(collective_id=1, has_side_effects=True),
    )(piece)
    return out.reshape(halves, strips, rows, chans)


def correlate_kernel(factor, x_ref, f_ref, o_ref, acc_ref):
    for s in range(x_ref.shape[0]):
        acc_ref[:, s, :] = jnp.dot(x_ref[s], f_ref[...], preferred_element_type=jnp.float32)
    o_ref[...] = (acc_ref[...] * factor).astype(o_ref.dtype)


def correlate(gathered, queries, factor, share, strips_per_step=32, rows_per_step=320):
    halves, strips, half_rows, chans = gathered.shape
    width = queries.shape[1]
    per_half = half_rows // rows_per_step
    grid = (pl.cdiv(share, rows_per_step), strips // strips_per_step)
    return pl.pallas_call(
        functools.partial(correlate_kernel, factor),
        out_shape=jax.ShapeDtypeStruct((share, strips, width), jnp.bfloat16),
        grid=grid,
        in_specs=[
            pl.BlockSpec(
                (None, strips_per_step, rows_per_step, chans),
                lambda i, j: (i // per_half, j, i % per_half, 0),
            ),
            pl.BlockSpec((chans, width), lambda i, j: (0, 0)),
        ],
        out_specs=pl.BlockSpec((rows_per_step, strips_per_step, width), lambda i, j: (i, j, 0)),
        scratch_shapes=[pltpu.VMEM((rows_per_step, strips_per_step, width), jnp.float32)],
        cost_estimate=pl.CostEstimate(
            flops=2 * strips * share * chans * width,
            bytes_accessed=2 * (strips * share * chans + width * chans + strips * share * width),
            transcendentals=0,
        ),
    )(gathered, queries)


def local(frame_one, frame_two):
    pooled = pool_strip(frame_two)
    groups = lax.axis_size("chan")
    channels = groups * frame_one.shape[1]
    factor = 1.0 / float(channels) ** 0.5
    strips = lax.axis_size("rows")
    share = pooled.shape[0] // groups
    slices = pooled.shape[1]
    blocks = jnp.transpose(pooled.reshape(groups, share, slices), (0, 2, 1))
    traded, pieces = trade(blocks, frame_one.T)
    weights = pieces.reshape(channels, frame_one.shape[0])
    traded = jnp.transpose(traded, (2, 0, 1)).reshape(share, channels)
    padded = -(-share // 320) * 320
    traded = jnp.pad(traded, ((0, padded - share), (0, 0)))
    gathered = gather(traded.reshape(2, padded // 2, channels), strips)
    values = correlate(gathered, weights, factor, share)
    return jnp.transpose(values, (1, 0, 2))


def solution(mesh):
    in_specs = (P("rows", "chan"), P("rows", None, "chan"))
    out_specs = P(None, "chan", "rows")
    return jax.shard_map(local, mesh=mesh, in_specs=in_specs, out_specs=out_specs, check_vma=False)
```

```python
import functools

import jax
import jax.numpy as jnp
from jax import lax
from jax.experimental import pallas as pl
from jax.experimental.pallas import tpu as pltpu
from jax.sharding import PartitionSpec as P

MESH_ID = pl.DeviceIdType.MESH


def pool_strip(strip):
    full = strip.astype(jnp.float32)
    rows_n, cols_n, chans = full.shape
    level_one = full.reshape(rows_n // 2, 2, cols_n // 2, 2, chans).mean(axis=(1, 3))
    level_two = level_one.reshape(rows_n // 4, 2, cols_n // 4, 2, chans).mean(axis=(1, 3))
    joined = jnp.concatenate(
        [full.reshape(-1, chans), level_one.reshape(-1, chans), level_two.reshape(-1, chans)],
        axis=0,
    )
    return joined.astype(jnp.bfloat16)


def trade_kernel(n, x_ref, f_ref, o_ref, g_ref, buf, fbuf, send_sem, recv_sem, fsend_sem, frecv_sem):
    me = lax.axis_index("chan")
    row = lax.axis_index("rows")
    barrier = pltpu.get_barrier_semaphore()
    for k in range(1, n):
        peer = lax.rem(me + k, n)
        pl.semaphore_signal(barrier, inc=1, device_id=(row, peer), device_id_type=MESH_ID)
    pl.semaphore_wait(barrier, n - 1)
    sends = []
    for k in range(1, n):
        peer = lax.rem(me + k, n)
        for src, dst, ssem, rsem in ((x_ref.at[peer], buf.at[me], send_sem, recv_sem), (f_ref, fbuf.at[me], fsend_sem, frecv_sem)):
            copy = pltpu.make_async_remote_copy(
                src_ref=src,
                dst_ref=dst,
                send_sem=ssem.at[k],
                recv_sem=rsem.at[k],
                device_id=(row, peer),
                device_id_type=MESH_ID,
            )
            copy.start()
            sends.append(copy)
    o_ref[me] = x_ref[me]
    g_ref[me] = f_ref[...]
    for k in range(1, n):
        source = lax.rem(me + n - k, n)
        for src, dst, ssem, rsem, out in ((x_ref.at[me], buf.at[source], send_sem, recv_sem, o_ref), (f_ref, fbuf.at[source], fsend_sem, frecv_sem, g_ref)):
            arrival = pltpu.make_async_remote_copy(
                src_ref=src,
                dst_ref=dst,
                send_sem=ssem.at[k],
                recv_sem=rsem.at[k],
                device_id=(row, source),
                device_id_type=MESH_ID,
            )
            arrival.wait_recv()
            out[source] = dst[...]
    for copy in sends:
        copy.wait_send()


def trade(blocks, piece):
    n = blocks.shape[0]
    gathered = (n,) + piece.shape
    return pl.pallas_call(
        functools.partial(trade_kernel, n),
        out_shape=(
            jax.ShapeDtypeStruct(blocks.shape, blocks.dtype),
            jax.ShapeDtypeStruct(gathered, piece.dtype),
        ),
        in_specs=[pl.BlockSpec(memory_space=pltpu.VMEM)] * 2,
        out_specs=(pl.BlockSpec(memory_space=pltpu.VMEM),) * 2,
        scratch_shapes=[
            pltpu.VMEM(blocks.shape, blocks.dtype),
            pltpu.VMEM(gathered, piece.dtype),
            pltpu.SemaphoreType.DMA((n,)),
            pltpu.SemaphoreType.DMA((n,)),
            pltpu.SemaphoreType.DMA((n,)),
            pltpu.SemaphoreType.DMA((n,)),
        ],
        compiler_params=pltpu.CompilerParams(collective_id=0, has_side_effects=True),
    )(blocks, piece)


def gather_kernel(zn, piece_ref, out_ref, send_sem, recv_sem, local_sem):
    row = lax.axis_index("rows")
    col = lax.axis_index("chan")
    b = row % 2
    ylo = (row // 2) % 2
    z = row // 4
    m = ylo * 2 + b
    other = 1 - ylo

    def device(zz, yy, cc):
        return (((zz % zn) * 2 + yy) * 2 + cc, col)

    partner = device(z, ylo, 1 - b)
    ups = device(z + 1, ylo, b)
    downs = device(z + zn - 1, ylo, b)
    side = [device(z, other, c) for c in range(2)]

    barrier = pltpu.get_barrier_semaphore()
    for peer in [partner, ups, downs] + side:
        pl.semaphore_signal(barrier, inc=1, device_id=peer, device_id_type=MESH_ID)
    pl.semaphore_wait(barrier, 5)

    def remote(src, dst, idx, peer, arrival=None):
        arrival = idx if arrival is None else arrival
        return pltpu.make_async_remote_copy(
            src_ref=src, dst_ref=dst, send_sem=send_sem.at[idx], recv_sem=recv_sem.at[arrival],
            device_id=peer, device_id_type=MESH_ID,
        )

    started = []

    def send(src, dst, idx, peer, arrival=None):
        copy = remote(src, dst, idx, peer, arrival)
        copy.start()
        started.append(copy)

    def arrive(dst, idx):
        remote(dst, dst, idx, partner).wait_recv()

    own = []
    for h in range(2):
        copy = pltpu.make_async_copy(piece_ref.at[h], out_ref.at[h, z, m], local_sem.at[h])
        copy.start()
        own.append(copy)
    for h in range(2):
        send(piece_ref.at[h], out_ref.at[h, z, m], h, partner)
    for c in range(2):
        send(piece_ref.at[c], out_ref.at[c, z, m], 2 + c, side[c], 4 + b)
    for copy in own:
        copy.wait()
    arrive(out_ref.at[b, z, ylo * 2 + 1 - b], b)
    arrive(out_ref.at[b, z, other * 2 + ylo], 4 + ylo)
    side_slots = pl.ds(other * 2, 2)

    steps = zn // 2
    rows = piece_ref.shape[1]
    carried = pl.ds(ylo, 3)
    lent = 3 * ylo
    wanted = 3 * other
    up_rows = pl.ds(0, rows // 2)
    down_rows = pl.ds(rows // 2, rows // 2)
    ring_regions = []

    def send_ring(up, t):
        if up:
            block = (z - (t - 1) + zn) % zn
            part, idx, peer = up_rows, 6, ups
        else:
            block = (z + (t - 1)) % zn
            part, idx, peer = down_rows, 10, downs
        if t < steps:
            src = out_ref.at[b, block, carried]
        else:
            src = out_ref.at[b, block, carried, part]
        send(src, src, idx + (t - 1), peer)

    send_ring(True, 1)
    send_ring(False, 1)
    arrive(out_ref.at[1 - b, z, ylo * 2 + 1 - b], 1 - b)
    arrive(out_ref.at[b, z, other * 2 + 1 - ylo], 5 - ylo)
    send(out_ref.at[b, z, side_slots], out_ref.at[b, z, side_slots], 22, partner)
    for t in range(1, steps + 1):
        got_up = (z - t + zn) % zn
        got_down = (z + t) % zn
        picks = [(True, got_up, 6, 14, 23, 31, up_rows), (False, got_down, 10, 18, 27, 35, down_rows)]
        for up, block, ring_idx, lend_idx, fwd_idx, fwd_lent_idx, part in picks:
            if t < steps:
                dst = out_ref.at[b, block, carried]
                lend = out_ref.at[b, block, lent]
            else:
                dst = out_ref.at[b, block, carried, part]
                lend = out_ref.at[b, block, lent, part]
            arrive(dst, ring_idx + (t - 1))
            if t < steps:
                send_ring(up, t + 1)
            send(lend, lend, lend_idx + (t - 1), device(z, other, b))
            send(dst, dst, fwd_idx + (t - 1), partner)
            ring_regions.append((block, part, ring_idx, lend_idx, fwd_idx, fwd_lent_idx, t))
    for block, part, ring_idx, lend_idx, fwd_idx, fwd_lent_idx, t in ring_regions:
        if t < steps:
            got = out_ref.at[b, block, wanted]
        else:
            got = out_ref.at[b, block, wanted, part]
        arrive(got, lend_idx + (t - 1))
        send(got, got, fwd_lent_idx + (t - 1), partner)

    arrive(out_ref.at[1 - b, z, side_slots], 22)
    for block, part, ring_idx, lend_idx, fwd_idx, fwd_lent_idx, t in ring_regions:
        if t < steps:
            dst = out_ref.at[1 - b, block, carried]
            got = out_ref.at[1 - b, block, wanted]
        else:
            dst = out_ref.at[1 - b, block, carried, part]
            got = out_ref.at[1 - b, block, wanted, part]
        arrive(dst, fwd_idx + (t - 1))
        arrive(got, fwd_lent_idx + (t - 1))
    for copy in started:
        copy.wait_send()


def gather(piece, strips):
    halves, rows, chans = piece.shape
    zn = strips // 4
    sems = 39
    out = pl.pallas_call(
        functools.partial(gather_kernel, zn),
        out_shape=jax.ShapeDtypeStruct((halves, zn, 4, rows, chans), piece.dtype),
        in_specs=[pl.BlockSpec(memory_space=pltpu.VMEM)],
        out_specs=pl.BlockSpec(memory_space=pl.ANY),
        scratch_shapes=[
            pltpu.SemaphoreType.DMA((sems,)),
            pltpu.SemaphoreType.DMA((sems,)),
            pltpu.SemaphoreType.DMA((2,)),
        ],
        compiler_params=pltpu.CompilerParams(collective_id=1, has_side_effects=True),
    )(piece)
    return out.reshape(halves, strips, rows, chans)


def correlate_kernel(factor, x_ref, f_ref, o_ref, acc_ref):
    for s in range(x_ref.shape[0]):
        acc_ref[:, s, :] = jnp.dot(x_ref[s], f_ref[...], preferred_element_type=jnp.float32)
    o_ref[...] = (acc_ref[...] * factor).astype(o_ref.dtype)


def correlate(gathered, queries, factor, share, strips_per_step=16, rows_per_step=320):
    halves, strips, half_rows, chans = gathered.shape
    width = queries.shape[1]
    per_half = half_rows // rows_per_step
    grid = (pl.cdiv(share, rows_per_step), strips // strips_per_step)
    return pl.pallas_call(
        functools.partial(correlate_kernel, factor),
        out_shape=jax.ShapeDtypeStruct((share, strips, width), jnp.bfloat16),
        grid=grid,
        in_specs=[
            pl.BlockSpec(
                (None, strips_per_step, rows_per_step, chans),
                lambda i, j: (i // per_half, j, i % per_half, 0),
            ),
            pl.BlockSpec((chans, width), lambda i, j: (0, 0)),
        ],
        out_specs=pl.BlockSpec((rows_per_step, strips_per_step, width), lambda i, j: (i, j, 0)),
        scratch_shapes=[pltpu.VMEM((rows_per_step, strips_per_step, width), jnp.float32)],
        cost_estimate=pl.CostEstimate(
            flops=2 * strips * share * chans * width,
            bytes_accessed=2 * (strips * share * chans + width * chans + strips * share * width),
            transcendentals=0,
        ),
    )(gathered, queries)


def local(frame_one, frame_two):
    pooled = pool_strip(frame_two)
    groups = lax.axis_size("chan")
    channels = groups * frame_one.shape[1]
    factor = 1.0 / float(channels) ** 0.5
    strips = lax.axis_size("rows")
    share = pooled.shape[0] // groups
    slices = pooled.shape[1]
    padded = -(-share // 320) * 320
    blocks = jnp.transpose(pooled.reshape(groups, share, slices), (0, 2, 1))
    blocks = jnp.pad(blocks, ((0, 0), (0, 0), (0, padded - share)))
    traded, pieces = trade(blocks, frame_one.T)
    weights = pieces.reshape(channels, frame_one.shape[0])
    traded = jnp.transpose(traded, (2, 0, 1)).reshape(padded, channels)
    gathered = gather(traded.reshape(2, padded // 2, channels), strips)
    values = correlate(gathered, weights, factor, share)
    return jnp.transpose(values, (1, 0, 2))


def solution(mesh):
    in_specs = (P("rows", "chan"), P("rows", None, "chan"))
    out_specs = P(None, "chan", "rows")
    return jax.shard_map(local, mesh=mesh, in_specs=in_specs, out_specs=out_specs, check_vma=False)
```

```python
import functools

import jax
import jax.numpy as jnp
from jax import lax
from jax.experimental import pallas as pl
from jax.experimental.pallas import tpu as pltpu
from jax.sharding import PartitionSpec as P

MESH_ID = pl.DeviceIdType.MESH


def pool_strip(strip):
    full = strip.astype(jnp.float32)
    rows_n, cols_n, chans = full.shape
    level_one = full.reshape(rows_n // 2, 2, cols_n // 2, 2, chans).mean(axis=(1, 3))
    level_two = level_one.reshape(rows_n // 4, 2, cols_n // 4, 2, chans).mean(axis=(1, 3))
    joined = jnp.concatenate(
        [full.reshape(-1, chans), level_one.reshape(-1, chans), level_two.reshape(-1, chans)],
        axis=0,
    )
    return joined.astype(jnp.bfloat16)


def trade_kernel(n, x_ref, f_ref, o_ref, g_ref, buf, fbuf, send_sem, recv_sem, fsend_sem, frecv_sem):
    me = lax.axis_index("chan")
    row = lax.axis_index("rows")
    barrier = pltpu.get_barrier_semaphore()
    for k in range(1, n):
        peer = lax.rem(me + k, n)
        pl.semaphore_signal(barrier, inc=1, device_id=(row, peer), device_id_type=MESH_ID)
    pl.semaphore_wait(barrier, n - 1)
    sends = []
    for k in range(1, n):
        peer = lax.rem(me + k, n)
        for src, dst, ssem, rsem in ((x_ref.at[peer], buf.at[me], send_sem, recv_sem), (f_ref, fbuf.at[me], fsend_sem, frecv_sem)):
            copy = pltpu.make_async_remote_copy(
                src_ref=src,
                dst_ref=dst,
                send_sem=ssem.at[k],
                recv_sem=rsem.at[k],
                device_id=(row, peer),
                device_id_type=MESH_ID,
            )
            copy.start()
            sends.append(copy)
    o_ref[me] = x_ref[me]
    g_ref[me] = f_ref[...]
    for k in range(1, n):
        source = lax.rem(me + n - k, n)
        for src, dst, ssem, rsem, out in ((x_ref.at[me], buf.at[source], send_sem, recv_sem, o_ref), (f_ref, fbuf.at[source], fsend_sem, frecv_sem, g_ref)):
            arrival = pltpu.make_async_remote_copy(
                src_ref=src,
                dst_ref=dst,
                send_sem=ssem.at[k],
                recv_sem=rsem.at[k],
                device_id=(row, source),
                device_id_type=MESH_ID,
            )
            arrival.wait_recv()
            out[source] = dst[...]
    for copy in sends:
        copy.wait_send()


def trade(blocks, piece):
    n = blocks.shape[0]
    gathered = (n,) + piece.shape
    return pl.pallas_call(
        functools.partial(trade_kernel, n),
        out_shape=(
            jax.ShapeDtypeStruct(blocks.shape, blocks.dtype),
            jax.ShapeDtypeStruct(gathered, piece.dtype),
        ),
        in_specs=[pl.BlockSpec(memory_space=pltpu.VMEM)] * 2,
        out_specs=(pl.BlockSpec(memory_space=pltpu.VMEM),) * 2,
        scratch_shapes=[
            pltpu.VMEM(blocks.shape, blocks.dtype),
            pltpu.VMEM(gathered, piece.dtype),
            pltpu.SemaphoreType.DMA((n,)),
            pltpu.SemaphoreType.DMA((n,)),
            pltpu.SemaphoreType.DMA((n,)),
            pltpu.SemaphoreType.DMA((n,)),
        ],
        compiler_params=pltpu.CompilerParams(collective_id=0, has_side_effects=True),
    )(blocks, piece)


def gather_kernel(zn, piece_ref, out_ref, send_sem, recv_sem, local_sem):
    row = lax.axis_index("rows")
    col = lax.axis_index("chan")
    b = row % 2
    ylo = (row // 2) % 2
    z = row // 4
    m = ylo * 2 + b
    other = 1 - ylo

    def device(zz, yy, cc):
        return (((zz % zn) * 2 + yy) * 2 + cc, col)

    partner = device(z, ylo, 1 - b)
    ups = device(z + 1, ylo, b)
    downs = device(z + zn - 1, ylo, b)
    side = [device(z, other, c) for c in range(2)]

    barrier = pltpu.get_barrier_semaphore()
    for peer in [partner, ups, downs] + side:
        pl.semaphore_signal(barrier, inc=1, device_id=peer, device_id_type=MESH_ID)
    pl.semaphore_wait(barrier, 5)

    def remote(src, dst, idx, peer, arrival=None):
        arrival = idx if arrival is None else arrival
        return pltpu.make_async_remote_copy(
            src_ref=src, dst_ref=dst, send_sem=send_sem.at[idx], recv_sem=recv_sem.at[arrival],
            device_id=peer, device_id_type=MESH_ID,
        )

    started = []

    def send(src, dst, idx, peer, arrival=None):
        copy = remote(src, dst, idx, peer, arrival)
        copy.start()
        started.append(copy)

    def arrive(dst, idx):
        remote(dst, dst, idx, partner).wait_recv()

    own = []
    for h in range(2):
        copy = pltpu.make_async_copy(piece_ref.at[h], out_ref.at[h, z, m], local_sem.at[h])
        copy.start()
        own.append(copy)
    for h in range(2):
        send(piece_ref.at[h], out_ref.at[h, z, m], h, partner)
    for c in range(2):
        send(piece_ref.at[c], out_ref.at[c, z, m], 2 + c, side[c], 4 + b)
    for copy in own:
        copy.wait()
    arrive(out_ref.at[b, z, ylo * 2 + 1 - b], b)
    arrive(out_ref.at[b, z, other * 2 + ylo], 4 + ylo)
    side_slots = pl.ds(other * 2, 2)

    steps = zn // 2
    rows = piece_ref.shape[1]
    carried = pl.ds(ylo, 3)
    lent = 3 * ylo
    wanted = 3 * other
    up_rows = pl.ds(0, rows // 2)
    down_rows = pl.ds(rows // 2, rows // 2)
    ring_regions = []

    def send_ring(up, t):
        if up:
            block = (z - (t - 1) + zn) % zn
            part, idx, peer = up_rows, 6, ups
        else:
            block = (z + (t - 1)) % zn
            part, idx, peer = down_rows, 10, downs
        if t < steps:
            src = out_ref.at[b, block, carried]
        else:
            src = out_ref.at[b, block, carried, part]
        send(src, src, idx + (t - 1), peer)

    send_ring(True, 1)
    send_ring(False, 1)
    arrive(out_ref.at[1 - b, z, ylo * 2 + 1 - b], 1 - b)
    arrive(out_ref.at[b, z, other * 2 + 1 - ylo], 5 - ylo)
    send(out_ref.at[b, z, side_slots], out_ref.at[b, z, side_slots], 22, partner)
    for t in range(1, steps + 1):
        got_up = (z - t + zn) % zn
        got_down = (z + t) % zn
        picks = [(True, got_up, 6, 14, 23, 31, up_rows), (False, got_down, 10, 18, 27, 35, down_rows)]
        for up, block, ring_idx, lend_idx, fwd_idx, fwd_lent_idx, part in picks:
            if t < steps:
                dst = out_ref.at[b, block, carried]
                lend = out_ref.at[b, block, lent]
            else:
                dst = out_ref.at[b, block, carried, part]
                lend = out_ref.at[b, block, lent, part]
            arrive(dst, ring_idx + (t - 1))
            if t < steps:
                send_ring(up, t + 1)
            send(lend, lend, lend_idx + (t - 1), device(z, other, b))
            send(dst, dst, fwd_idx + (t - 1), partner)
            ring_regions.append((block, part, ring_idx, lend_idx, fwd_idx, fwd_lent_idx, t))
    for block, part, ring_idx, lend_idx, fwd_idx, fwd_lent_idx, t in ring_regions:
        if t < steps:
            got = out_ref.at[b, block, wanted]
        else:
            got = out_ref.at[b, block, wanted, part]
        arrive(got, lend_idx + (t - 1))
        send(got, got, fwd_lent_idx + (t - 1), partner)

    arrive(out_ref.at[1 - b, z, side_slots], 22)
    for block, part, ring_idx, lend_idx, fwd_idx, fwd_lent_idx, t in ring_regions:
        if t < steps:
            dst = out_ref.at[1 - b, block, carried]
            got = out_ref.at[1 - b, block, wanted]
        else:
            dst = out_ref.at[1 - b, block, carried, part]
            got = out_ref.at[1 - b, block, wanted, part]
        arrive(dst, fwd_idx + (t - 1))
        arrive(got, fwd_lent_idx + (t - 1))
    for copy in started:
        copy.wait_send()


def gather(piece, strips):
    halves, rows, chans = piece.shape
    zn = strips // 4
    sems = 39
    out = pl.pallas_call(
        functools.partial(gather_kernel, zn),
        out_shape=jax.ShapeDtypeStruct((halves, zn, 4, rows, chans), piece.dtype),
        in_specs=[pl.BlockSpec(memory_space=pltpu.VMEM)],
        out_specs=pl.BlockSpec(memory_space=pl.ANY),
        scratch_shapes=[
            pltpu.SemaphoreType.DMA((sems,)),
            pltpu.SemaphoreType.DMA((sems,)),
            pltpu.SemaphoreType.DMA((2,)),
        ],
        compiler_params=pltpu.CompilerParams(collective_id=1, has_side_effects=True),
    )(piece)
    return out.reshape(halves, strips, rows, chans)


def correlate_kernel(factor, x_ref, f_ref, o_ref, acc_ref):
    for s in range(x_ref.shape[0]):
        acc_ref[:, s, :] = jnp.dot(x_ref[s], f_ref[...], preferred_element_type=jnp.float32)
    o_ref[...] = (acc_ref[...] * factor).astype(o_ref.dtype)


def correlate(gathered, queries, factor, share, strips_per_step=8, rows_per_step=320):
    halves, strips, half_rows, chans = gathered.shape
    width = queries.shape[1]
    per_half = half_rows // rows_per_step
    grid = (pl.cdiv(share, rows_per_step), strips // strips_per_step)
    return pl.pallas_call(
        functools.partial(correlate_kernel, factor),
        out_shape=jax.ShapeDtypeStruct((share, strips, width), jnp.bfloat16),
        grid=grid,
        in_specs=[
            pl.BlockSpec(
                (None, strips_per_step, rows_per_step, chans),
                lambda i, j: (i // per_half, j, i % per_half, 0),
            ),
            pl.BlockSpec((chans, width), lambda i, j: (0, 0)),
        ],
        out_specs=pl.BlockSpec((rows_per_step, strips_per_step, width), lambda i, j: (i, j, 0)),
        scratch_shapes=[pltpu.VMEM((rows_per_step, strips_per_step, width), jnp.float32)],
        cost_estimate=pl.CostEstimate(
            flops=2 * strips * share * chans * width,
            bytes_accessed=2 * (strips * share * chans + width * chans + strips * share * width),
            transcendentals=0,
        ),
    )(gathered, queries)


def local(frame_one, frame_two):
    pooled = pool_strip(frame_two)
    groups = lax.axis_size("chan")
    channels = groups * frame_one.shape[1]
    factor = 1.0 / float(channels) ** 0.5
    strips = lax.axis_size("rows")
    share = pooled.shape[0] // groups
    slices = pooled.shape[1]
    padded = -(-share // 320) * 320
    blocks = jnp.transpose(pooled.reshape(groups, share, slices), (0, 2, 1))
    blocks = jnp.pad(blocks, ((0, 0), (0, 0), (0, padded - share)))
    traded, pieces = trade(blocks, frame_one.T)
    weights = pieces.reshape(channels, frame_one.shape[0])
    traded = jnp.transpose(traded, (2, 0, 1)).reshape(padded, channels)
    gathered = gather(traded.reshape(2, padded // 2, channels), strips)
    values = correlate(gathered, weights, factor, share)
    return jnp.transpose(values, (1, 0, 2))


def solution(mesh):
    in_specs = (P("rows", "chan"), P("rows", None, "chan"))
    out_specs = P(None, "chan", "rows")
    return jax.shard_map(local, mesh=mesh, in_specs=in_specs, out_specs=out_specs, check_vma=False)
```

```python
import functools

import jax
import jax.numpy as jnp
from jax import lax
from jax.experimental import pallas as pl
from jax.experimental.pallas import tpu as pltpu
from jax.sharding import PartitionSpec as P

MESH_ID = pl.DeviceIdType.MESH


def pool_strip(strip):
    full = strip.astype(jnp.float32)
    rows_n, cols_n, chans = full.shape
    level_one = full.reshape(rows_n // 2, 2, cols_n // 2, 2, chans).mean(axis=(1, 3))
    level_two = level_one.reshape(rows_n // 4, 2, cols_n // 4, 2, chans).mean(axis=(1, 3))
    joined = jnp.concatenate(
        [full.reshape(-1, chans), level_one.reshape(-1, chans), level_two.reshape(-1, chans)],
        axis=0,
    )
    return joined.astype(jnp.bfloat16)


def trade_kernel(n, x_ref, f_ref, o_ref, g_ref, buf, fbuf, send_sem, recv_sem, fsend_sem, frecv_sem):
    me = lax.axis_index("chan")
    row = lax.axis_index("rows")
    barrier = pltpu.get_barrier_semaphore()
    for k in range(1, n):
        peer = lax.rem(me + k, n)
        pl.semaphore_signal(barrier, inc=1, device_id=(row, peer), device_id_type=MESH_ID)
    pl.semaphore_wait(barrier, n - 1)
    sends = []
    for k in range(1, n):
        peer = lax.rem(me + k, n)
        for src, dst, ssem, rsem in ((x_ref.at[peer], buf.at[me], send_sem, recv_sem), (f_ref, fbuf.at[me], fsend_sem, frecv_sem)):
            copy = pltpu.make_async_remote_copy(
                src_ref=src,
                dst_ref=dst,
                send_sem=ssem.at[k],
                recv_sem=rsem.at[k],
                device_id=(row, peer),
                device_id_type=MESH_ID,
            )
            copy.start()
            sends.append(copy)
    o_ref[me] = x_ref[me]
    g_ref[me] = f_ref[...]
    for k in range(1, n):
        source = lax.rem(me + n - k, n)
        for src, dst, ssem, rsem, out in ((x_ref.at[me], buf.at[source], send_sem, recv_sem, o_ref), (f_ref, fbuf.at[source], fsend_sem, frecv_sem, g_ref)):
            arrival = pltpu.make_async_remote_copy(
                src_ref=src,
                dst_ref=dst,
                send_sem=ssem.at[k],
                recv_sem=rsem.at[k],
                device_id=(row, source),
                device_id_type=MESH_ID,
            )
            arrival.wait_recv()
            out[source] = dst[...]
    for copy in sends:
        copy.wait_send()


def trade(blocks, piece):
    n = blocks.shape[0]
    gathered = (n,) + piece.shape
    return pl.pallas_call(
        functools.partial(trade_kernel, n),
        out_shape=(
            jax.ShapeDtypeStruct(blocks.shape, blocks.dtype),
            jax.ShapeDtypeStruct(gathered, piece.dtype),
        ),
        in_specs=[pl.BlockSpec(memory_space=pltpu.VMEM)] * 2,
        out_specs=(pl.BlockSpec(memory_space=pltpu.VMEM),) * 2,
        scratch_shapes=[
            pltpu.VMEM(blocks.shape, blocks.dtype),
            pltpu.VMEM(gathered, piece.dtype),
            pltpu.SemaphoreType.DMA((n,)),
            pltpu.SemaphoreType.DMA((n,)),
            pltpu.SemaphoreType.DMA((n,)),
            pltpu.SemaphoreType.DMA((n,)),
        ],
        compiler_params=pltpu.CompilerParams(collective_id=0, has_side_effects=True),
    )(blocks, piece)


def gather_kernel(zn, piece_ref, out_ref, send_sem, recv_sem, local_sem):
    row = lax.axis_index("rows")
    col = lax.axis_index("chan")
    b = row % 2
    ylo = (row // 2) % 2
    z = row // 4
    m = ylo * 2 + b
    other = 1 - ylo

    def device(zz, yy, cc):
        return (((zz % zn) * 2 + yy) * 2 + cc, col)

    partner = device(z, ylo, 1 - b)
    ups = device(z + 1, ylo, b)
    downs = device(z + zn - 1, ylo, b)
    side = [device(z, other, c) for c in range(2)]

    barrier = pltpu.get_barrier_semaphore()
    for peer in [partner, ups, downs] + side:
        pl.semaphore_signal(barrier, inc=1, device_id=peer, device_id_type=MESH_ID)
    pl.semaphore_wait(barrier, 5)

    def remote(src, dst, idx, peer, arrival=None):
        arrival = idx if arrival is None else arrival
        return pltpu.make_async_remote_copy(
            src_ref=src, dst_ref=dst, send_sem=send_sem.at[idx], recv_sem=recv_sem.at[arrival],
            device_id=peer, device_id_type=MESH_ID,
        )

    started = []

    def send(src, dst, idx, peer, arrival=None):
        copy = remote(src, dst, idx, peer, arrival)
        copy.start()
        started.append(copy)

    def arrive(dst, idx):
        remote(dst, dst, idx, partner).wait_recv()

    own = []
    for h in range(2):
        copy = pltpu.make_async_copy(piece_ref.at[h], out_ref.at[h, z, m], local_sem.at[h])
        copy.start()
        own.append(copy)
    for c in range(2):
        send(piece_ref.at[c], out_ref.at[c, z, m], 2 + c, side[c], 4 + b)
    for h in range(2):
        send(piece_ref.at[h], out_ref.at[h, z, m], h, partner)
    for copy in own:
        copy.wait()
    arrive(out_ref.at[b, z, ylo * 2 + 1 - b], b)
    arrive(out_ref.at[b, z, other * 2 + ylo], 4 + ylo)
    side_slots = pl.ds(other * 2, 2)

    steps = zn // 2
    rows = piece_ref.shape[1]
    carried = pl.ds(ylo, 3)
    lent = 3 * ylo
    wanted = 3 * other
    up_rows = pl.ds(0, rows // 2)
    down_rows = pl.ds(rows // 2, rows // 2)
    ring_regions = []

    def send_ring(up, t):
        if up:
            block = (z - (t - 1) + zn) % zn
            part, idx, peer = up_rows, 6, ups
        else:
            block = (z + (t - 1)) % zn
            part, idx, peer = down_rows, 10, downs
        if t < steps:
            src = out_ref.at[b, block, carried]
        else:
            src = out_ref.at[b, block, carried, part]
        send(src, src, idx + (t - 1), peer)

    send_ring(True, 1)
    send_ring(False, 1)
    arrive(out_ref.at[1 - b, z, ylo * 2 + 1 - b], 1 - b)
    arrive(out_ref.at[b, z, other * 2 + 1 - ylo], 5 - ylo)
    send(out_ref.at[b, z, side_slots], out_ref.at[b, z, side_slots], 22, partner)
    for t in range(1, steps + 1):
        got_up = (z - t + zn) % zn
        got_down = (z + t) % zn
        picks = [(True, got_up, 6, 14, 23, 31, up_rows), (False, got_down, 10, 18, 27, 35, down_rows)]
        for up, block, ring_idx, lend_idx, fwd_idx, fwd_lent_idx, part in picks:
            if t < steps:
                dst = out_ref.at[b, block, carried]
                lend = out_ref.at[b, block, lent]
            else:
                dst = out_ref.at[b, block, carried, part]
                lend = out_ref.at[b, block, lent, part]
            arrive(dst, ring_idx + (t - 1))
            if t < steps:
                send_ring(up, t + 1)
            send(lend, lend, lend_idx + (t - 1), device(z, other, b))
            send(dst, dst, fwd_idx + (t - 1), partner)
            ring_regions.append((block, part, ring_idx, lend_idx, fwd_idx, fwd_lent_idx, t))
    for block, part, ring_idx, lend_idx, fwd_idx, fwd_lent_idx, t in ring_regions:
        if t < steps:
            got = out_ref.at[b, block, wanted]
        else:
            got = out_ref.at[b, block, wanted, part]
        arrive(got, lend_idx + (t - 1))
        send(got, got, fwd_lent_idx + (t - 1), partner)

    arrive(out_ref.at[1 - b, z, side_slots], 22)
    for block, part, ring_idx, lend_idx, fwd_idx, fwd_lent_idx, t in ring_regions:
        if t < steps:
            dst = out_ref.at[1 - b, block, carried]
            got = out_ref.at[1 - b, block, wanted]
        else:
            dst = out_ref.at[1 - b, block, carried, part]
            got = out_ref.at[1 - b, block, wanted, part]
        arrive(dst, fwd_idx + (t - 1))
        arrive(got, fwd_lent_idx + (t - 1))
    for copy in started:
        copy.wait_send()


def gather(piece, strips):
    halves, rows, chans = piece.shape
    zn = strips // 4
    sems = 39
    out = pl.pallas_call(
        functools.partial(gather_kernel, zn),
        out_shape=jax.ShapeDtypeStruct((halves, zn, 4, rows, chans), piece.dtype),
        in_specs=[pl.BlockSpec(memory_space=pltpu.VMEM)],
        out_specs=pl.BlockSpec(memory_space=pl.ANY),
        scratch_shapes=[
            pltpu.SemaphoreType.DMA((sems,)),
            pltpu.SemaphoreType.DMA((sems,)),
            pltpu.SemaphoreType.DMA((2,)),
        ],
        compiler_params=pltpu.CompilerParams(collective_id=1, has_side_effects=True),
    )(piece)
    return out.reshape(halves, strips, rows, chans)


def correlate_kernel(factor, x_ref, f_ref, o_ref, acc_ref):
    for s in range(x_ref.shape[0]):
        acc_ref[:, s, :] = jnp.dot(x_ref[s], f_ref[...], preferred_element_type=jnp.float32)
    o_ref[...] = (acc_ref[...] * factor).astype(o_ref.dtype)


def correlate(gathered, queries, factor, share, strips_per_step=16, rows_per_step=320):
    halves, strips, half_rows, chans = gathered.shape
    width = queries.shape[1]
    per_half = half_rows // rows_per_step
    grid = (pl.cdiv(share, rows_per_step), strips // strips_per_step)
    return pl.pallas_call(
        functools.partial(correlate_kernel, factor),
        out_shape=jax.ShapeDtypeStruct((share, strips, width), jnp.bfloat16),
        grid=grid,
        in_specs=[
            pl.BlockSpec(
                (None, strips_per_step, rows_per_step, chans),
                lambda i, j: (i // per_half, j, i % per_half, 0),
            ),
            pl.BlockSpec((chans, width), lambda i, j: (0, 0)),
        ],
        out_specs=pl.BlockSpec((rows_per_step, strips_per_step, width), lambda i, j: (i, j, 0)),
        scratch_shapes=[pltpu.VMEM((rows_per_step, strips_per_step, width), jnp.float32)],
        cost_estimate=pl.CostEstimate(
            flops=2 * strips * share * chans * width,
            bytes_accessed=2 * (strips * share * chans + width * chans + strips * share * width),
            transcendentals=0,
        ),
    )(gathered, queries)


def local(frame_one, frame_two):
    pooled = pool_strip(frame_two)
    groups = lax.axis_size("chan")
    channels = groups * frame_one.shape[1]
    factor = 1.0 / float(channels) ** 0.5
    strips = lax.axis_size("rows")
    share = pooled.shape[0] // groups
    slices = pooled.shape[1]
    padded = -(-share // 320) * 320
    blocks = jnp.transpose(pooled.reshape(groups, share, slices), (0, 2, 1))
    blocks = jnp.pad(blocks, ((0, 0), (0, 0), (0, padded - share)))
    traded, pieces = trade(blocks, frame_one.T)
    weights = pieces.reshape(channels, frame_one.shape[0])
    traded = jnp.transpose(traded, (2, 0, 1)).reshape(padded, channels)
    gathered = gather(traded.reshape(2, padded // 2, channels), strips)
    values = correlate(gathered, weights, factor, share)
    return jnp.transpose(values, (1, 0, 2))


def solution(mesh):
    in_specs = (P("rows", "chan"), P("rows", None, "chan"))
    out_specs = P(None, "chan", "rows")
    return jax.shard_map(local, mesh=mesh, in_specs=in_specs, out_specs=out_specs, check_vma=False)
```
